256 devices in a mesh: grp: 64 (over y, x, z_lo, core), band: 4 (over z_hi).
Axes of the slice: x: 4, y: 4, z: 8 (z_hi: 4, z_lo: 2; z = z_hi * 2 + z_lo), core: 2. Of those that a mesh axis runs over, the one named last changes fastest.
Arguments:
- voltages: bfloat16 [64, 2048, 2048], P('band', 'grp'), may hold values from -6 to 6
- steering: int32 [2, 1024], replicated, may hold values from 0 to 255, as said below
- chan_sub: int32 [1024], P('band'), may hold values from 0 to 15, as said below
- delays: int32 [512, 16], P(None, 'band'), may hold values from 0 to 63
Outputs:
- dedispersed: float32 [64, 1024, 512], P(None, 'grp', 'band')
The draws below stay inside these ranges and needn't reach their ends.
Inputs may be any that keep to these rules, and one draw needn't show every extreme that they name: Every pair (steering[0, b], steering[1, b]) with the first below 256 and the second below 4 occurs for exactly one beam b. chan_sub[c] // 4 == c // 256: a channel belongs to a subband of its own quarter of the band.
All inputs are finite; a program needn't handle non-finite values.
Results may differ from the reference program's by a relative error of at most 0.0041.
Values may be sent and summed in bfloat16 or wider, within the bound.
No kernel may reach another device: no remote copies, remote signals or barrier semaphores. Data moves between devices by JAX's collectives and lax.ppermute only.
A program may use at most 64 MiB of HBM per device.

```python
import math
import jax
import jax.numpy as jnp
from jax import lax

A = 2048
FEEDS = 1024
NS_FEEDS = 256
C = 1024
SAMP = 2048
BEAMS = 1024
TRIALS = 512
SUB = 16
FR = 64
CQ = 256
SUBQ = 4


def draw_steering(key, part):
    shuffled = jax.random.permutation(key, BEAMS).astype(jnp.int32)
    north_ids = shuffled % NS_FEEDS
    east_ids = shuffled // NS_FEEDS % 4
    return jnp.stack([north_ids, east_ids]).astype(jnp.int32)


def draw_chan_sub(key, part):
    quarter_base = jnp.arange(C, dtype=jnp.int32) // CQ * SUBQ
    offsets = jax.random.randint(key, (C,), 0, SUBQ, dtype=jnp.int32)
    return (quarter_base + offsets).astype(jnp.int32)


def plant(array, key, smallest, top_value):
    place = [jax.random.randint(jax.random.fold_in(key, axis), (), 0, length) for axis, length in enumerate(array.shape)]
    widest = array.shape.index(max(array.shape))
    neighbour = place[:widest] + [(place[widest] + 1) % array.shape[widest]] + place[widest + 1:]
    return array.at[tuple(place)].set(smallest).at[tuple(neighbour)].set(top_value)


def block_scale(key, extent, pieces, smallest, top_value):
    factor_of, own = 1.0, jax.random.fold_in(key, 6)
    for position, blocks in pieces:
        draws = jnp.exp(jax.random.uniform(jax.random.fold_in(own, position), (blocks,), jnp.float32, smallest / len(pieces), top_value / len(pieces)))
        factor_of = factor_of * jnp.repeat(draws, extent[position] // blocks).reshape([-1 if axis == position else 1 for axis in range(len(extent))])
    return factor_of


def noise(key, shape, width, most, split=(), kind=jnp.bfloat16):
    gain = block_scale(key, shape, split, -0.22, 0.18) if split else 1.0
    result = jax.random.normal(key, shape, jnp.float32) * width * gain
    return jnp.minimum(jnp.maximum(result, -most), most).astype(kind)


def setup_inputs(seed: int = 0) -> dict:
    seeds = jax.random.split(jax.random.key(seed), 5)
    voltages = noise(seeds[0], (FR, A, SAMP), 1.0, 6.0, ((0, 4), (1, 64)))
    steering = draw_steering(jax.random.fold_in(seeds[4], 71), 0)
    chan_sub = draw_chan_sub(jax.random.fold_in(seeds[4], 71), 0)
    delays = plant(jax.random.randint(seeds[3], (TRIALS, SUB), 0, FR), jax.random.fold_in(seeds[3], 1), 0, FR - 1).astype(jnp.int32)
    return dict(voltages=voltages, steering=steering, chan_sub=chan_sub, delays=delays)


def window_taps():
    tap_pos = jnp.arange(4 * SAMP, dtype=jnp.float32) + 0.5
    hann_taper = 0.5 - 0.5 * jnp.cos(2.0 * math.pi / (4 * SAMP) * tap_pos)
    window = hann_taper * jnp.sinc((tap_pos - 2 * SAMP) / SAMP)
    window = window * jnp.sqrt(SAMP / jnp.sum(window * window))
    return window.reshape(4, SAMP)

def dft_table():
    row_ids = jnp.arange(SAMP, dtype=jnp.int32)
    col_ids = jnp.arange(SAMP, dtype=jnp.int32)
    chan_ids = row_ids % C
    phase_steps = chan_ids[:, None] * col_ids[None, :] % SAMP
    angles = 2.0 * math.pi / SAMP * phase_steps.astype(jnp.float32)
    row_scale = 1.0 / math.sqrt(SAMP)
    table = jnp.where((row_ids < C)[:, None], jnp.cos(angles), -jnp.sin(angles)) * row_scale
    return table.astype(jnp.bfloat16)

def beam_weights(channel_at, steering):
    feed_ids = jnp.arange(FEEDS, dtype=jnp.int32)
    north_pos = (feed_ids % NS_FEEDS).astype(jnp.float32) / NS_FEEDS
    east_pos = (feed_ids // NS_FEEDS).astype(jnp.float32) / 4.0
    geometry = north_pos[:, None] * steering[0][None, :].astype(jnp.float32) + east_pos[:, None] * steering[1][None, :].astype(jnp.float32)
    frequency = 1.0 - channel_at.astype(jnp.float32) / (2 * C)
    phases = 2.0 * math.pi * frequency * geometry
    weight_norm = 1.0 / math.sqrt(FEEDS)
    return jnp.concatenate([jnp.cos(phases) * weight_norm, jnp.sin(phases) * weight_norm], axis=1).astype(jnp.bfloat16)

def intensity(channel_block, weights):
    frames = channel_block.shape[1]
    input_rows = channel_block.reshape(4 * frames, FEEDS)
    products = jnp.dot(input_rows, weights, preferred_element_type=jnp.float32).reshape(2, frames, 2, 2, BEAMS)
    beam_re = products[0, :, :, 0] - products[1, :, :, 1]
    beam_im = products[0, :, :, 1] + products[1, :, :, 0]
    return lax.optimization_barrier(jnp.sum(beam_re * beam_re + beam_im * beam_im, axis=1)).astype(jnp.bfloat16)

def fourier_tables(total_frames):
    half_frames = total_frames // 2
    freq_ids = jnp.arange(1, half_frames + 1, dtype=jnp.int32)
    time_ids = jnp.arange(total_frames, dtype=jnp.int32)
    angles = 2.0 * math.pi / total_frames * (freq_ids[:, None] * time_ids[None, :] % total_frames).astype(jnp.float32)
    cosines = jnp.cos(angles)
    sines = jnp.sin(angles)
    forward = jnp.concatenate([cosines, -sines], axis=0)
    weight = jnp.where(freq_ids == half_frames, 1.0, 2.0).astype(jnp.float32) / (total_frames * math.sqrt(C))
    inverse = jnp.transpose(jnp.concatenate([cosines * weight[:, None], -sines * weight[:, None]], axis=0))
    return (forward, inverse)

def trial_phases(delays, total_frames):
    freq_ids = jnp.arange(1, total_frames // 2 + 1, dtype=jnp.int32)
    phase_steps = freq_ids[:, None, None] * jnp.transpose(delays)[None, :, :] % total_frames
    angles = 2.0 * math.pi / total_frames * phase_steps.astype(jnp.float32)
    return (jnp.cos(angles), jnp.sin(angles))

def dedisperse(centered, delays, total_frames):
    highest = lax.Precision.HIGHEST
    forward, inverse = fourier_tables(total_frames)
    half_frames = total_frames // 2
    spectrum = jnp.einsum('km,smb->ksb', forward, centered, precision=highest)
    spec_re = spectrum[:half_frames]
    spec_im = spectrum[half_frames:]
    cosines, sines = trial_phases(delays, total_frames)
    shifted_re = jnp.einsum('ksb,ksd->kbd', spec_re, cosines, precision=highest) + jnp.einsum('ksb,ksd->kbd', spec_im, sines, precision=highest)
    shifted_im = jnp.einsum('ksb,ksd->kbd', spec_im, cosines, precision=highest) - jnp.einsum('ksb,ksd->kbd', spec_re, sines, precision=highest)
    stacked = jnp.concatenate([shifted_re, shifted_im], axis=0)
    beams_here = centered.shape[2]
    trials_all = delays.shape[0]
    flattened = jnp.dot(inverse, stacked.reshape(2 * half_frames, beams_here * trials_all), precision=highest, preferred_element_type=jnp.float32)
    return flattened.reshape(total_frames, beams_here, trials_all)

def reference(voltages, steering, chan_sub, delays):
    total_frames = voltages.shape[0]
    window = window_taps()
    table = dft_table()
    padded = jnp.concatenate([jnp.zeros((3, A, SAMP), voltages.dtype), voltages], axis=0)

    def one_frame(frame_at):
        piece = lax.dynamic_slice_in_dim(padded, frame_at, 4, 0).astype(jnp.float32)
        filtered = window[0][None, :] * piece[0]
        for tap_at in range(1, 4):
            filtered = filtered + window[tap_at][None, :] * piece[tap_at]
        return lax.dot_general(table, filtered.astype(jnp.bfloat16), (((1,), (1,)), ((), ())), preferred_element_type=jnp.float32).astype(jnp.bfloat16)
    spectra = lax.map(one_frame, jnp.arange(total_frames, dtype=jnp.int32))

    def one_channel(channel_at):
        real_rows = lax.dynamic_index_in_dim(spectra, channel_at, 1, keepdims=False)
        imag_rows = lax.dynamic_index_in_dim(spectra, channel_at + C, 1, keepdims=False)
        channel_block = jnp.stack([real_rows, imag_rows])
        return intensity(channel_block, beam_weights(channel_at, steering))
    beam_power = lax.map(one_channel, jnp.arange(C, dtype=jnp.int32))
    member = (chan_sub[:, None] == jnp.arange(SUB, dtype=jnp.int32)[None, :]).astype(jnp.bfloat16)
    band_sums = jnp.dot(jnp.transpose(member), beam_power.reshape(C, total_frames * BEAMS), preferred_element_type=jnp.float32)
    band_sums = band_sums.reshape(SUB, total_frames, BEAMS)
    centered = band_sums - lax.optimization_barrier(jnp.mean(band_sums, axis=1, keepdims=True))
    return dedisperse(centered, delays, total_frames)
```

```python
import math

import jax
import jax.numpy as jnp
import numpy as np
from jax import lax
from jax.experimental import pallas as pl
from jax.experimental.pallas import tpu as pltpu
from jax.sharding import PartitionSpec as P

A = 2048
FEEDS = 1024
C = 1024
SAMP = 2048
BEAMS = 1024
TRIALS = 512
F32 = jnp.float32
BF16 = jnp.bfloat16
NT = (((1,), (1,)), ((), ()))
NN = (((1,), (0,)), ((), ()))


def window_taps():
    tap_pos = np.arange(4 * SAMP) + 0.5
    taper = 0.5 - 0.5 * np.cos(2.0 * np.pi / (4 * SAMP) * tap_pos)
    window = taper * np.sinc((tap_pos - 2 * SAMP) / SAMP)
    window = window * np.sqrt(SAMP / np.sum(window * window))
    return window.reshape(4, SAMP).astype(np.float32)


def lane_tables():
    r = np.arange(16)[:, None, None]
    k = np.arange(64)[None, :, None]
    lane = np.arange(128)[None, None, :]
    angle = 2.0 * np.pi / SAMP * (((16 * k + r) * lane) % SAMP)
    cos, sin = np.cos(angle) / np.sqrt(SAMP), np.sin(angle) / np.sqrt(SAMP)
    sign = np.where(r > 8, -1.0, 1.0)
    top = np.concatenate([cos, -sin * sign], axis=2)
    low = np.concatenate([-sin, -cos * sign], axis=2)
    return np.concatenate([top, low], axis=1).astype(jnp.bfloat16)


def real_dft16(x):
    h, c1, c3 = math.sqrt(0.5), math.cos(math.pi / 8), math.cos(3 * math.pi / 8)
    s = [x[j] + x[j + 8] for j in range(8)]
    d = [x[j] - x[j + 8] for j in range(8)]
    ss = [s[j] + s[j + 4] for j in range(4)]
    sd = [s[j] - s[j + 4] for j in range(4)]
    t0, t1 = ss[0] + ss[2], ss[1] + ss[3]
    out = [None] * 9
    out[0] = (t0 + t1, None)
    out[8] = (t0 - t1, None)
    out[4] = (ss[0] - ss[2], ss[1] - ss[3])
    dif, tot = h * (sd[1] - sd[3]), h * (sd[1] + sd[3])
    out[2] = (sd[0] + dif, sd[2] + tot)
    out[6] = (sd[0] - dif, tot - sd[2])
    p = [None] + [d[j] - d[8 - j] for j in (1, 2, 3)]
    q = [None] + [d[j] + d[8 - j] for j in (1, 2, 3)]
    hp, hq = h * p[2], h * q[2]
    ea, eb = d[0] + hp, d[0] - hp
    u, v = c1 * p[1] + c3 * p[3], c3 * p[1] - c1 * p[3]
    fa, fb = d[4] + hq, hq - d[4]
    y, z = c3 * q[1] + c1 * q[3], c1 * q[1] - c3 * q[3]
    out[1] = (ea + u, y + fa)
    out[7] = (ea - u, y - fa)
    out[3] = (eb + v, z + fb)
    out[5] = (eb - v, z - fb)
    return out


def spectra_kernel(v_ref, halo_ref, win_ref, tab_ref, out_ref, part_ref, turn_ref):
    frames = v_ref.shape[0]

    def bins(m, half, rows):
        a0 = 16 * half
        lanes = []
        for jb in range(16):
            cols = slice(128 * jb, 128 * jb + 128)
            total = None
            for p in range(4):
                term = rows(p)[pl.ds(a0, 16), cols].astype(F32) * win_ref[p : p + 1, cols]
                total = term if total is None else total + term
            lanes.append(total)
        row0 = pl.multiple_of(m * 32 + a0, 16)
        for at, (re, im) in enumerate(real_dft16(lanes)):
            part_ref[at, pl.ds(row0, 16), 0:128] = re.astype(BF16)
            if im is None:
                part_ref[at, pl.ds(row0, 16), 128:256] = jnp.zeros((16, 128), BF16)
            else:
                part_ref[at, pl.ds(row0, 16), 128:256] = im.astype(BF16)

    for m in range(3):
        for half in range(2):
            bins(m, half, lambda p, m=m: halo_ref.at[m + p] if m + p < 3 else v_ref.at[m + p - 3])

    def body(step, carry):
        m = step // 2
        bins(m, pl.multiple_of(step % 2, 1), lambda p: v_ref.at[m - 3 + p])
        return carry

    lax.fori_loop(6, 2 * frames, body, 0)

    def transform(r, carry):
        at = jnp.minimum(r, 16 - r)
        rows = lax.dot_general(tab_ref[r], part_ref[at], NT, preferred_element_type=F32)
        for reim in range(2):
            for mb in range(4):
                turn_ref[pl.ds(reim * 4 + mb, 64, stride=8), :] = rows[
                    64 * reim : 64 * reim + 64, 128 * mb : 128 * mb + 128
                ]
        for q in range(4):
            out_ref[q, r] = turn_ref[128 * q : 128 * q + 128, :].astype(BF16)
        return carry

    lax.fori_loop(0, 16, transform, 0)


def spectra(voltages, halo):
    return pl.pallas_call(
        spectra_kernel,
        out_shape=jax.ShapeDtypeStruct((4, 16, 128, 128), BF16),
        in_specs=[pl.BlockSpec(memory_space=pltpu.VMEM)] * 4,
        out_specs=pl.BlockSpec(memory_space=pltpu.VMEM),
        scratch_shapes=[pltpu.VMEM((9, 512, 256), BF16), pltpu.VMEM((512, 128), F32)],
        cost_estimate=pl.CostEstimate(
            flops=600_000_000, bytes_accessed=6_000_000, transcendentals=0
        ),
    )(voltages, halo, jnp.asarray(window_taps()), jnp.asarray(lane_tables()))


def turn_blocks(tiles):
    lane = lax.broadcasted_iota(jnp.int32, tiles[0].shape, 1)
    odd, high = (lane // 32) % 2 == 1, lane // 64 == 1
    one = [None] * 4
    for a, b in ((0, 1), (2, 3)):
        one[a] = jnp.where(odd, pltpu.roll(tiles[b], 32, 1), tiles[a])
        one[b] = jnp.where(odd, tiles[b], pltpu.roll(tiles[a], 96, 1))
    two = [None] * 4
    for a, b in ((0, 2), (1, 3)):
        two[a] = jnp.where(high, pltpu.roll(one[b], 64, 1), one[a])
        two[b] = jnp.where(high, one[b], pltpu.roll(one[a], 64, 1))
    return two


def beam_kernel(east_ref, sub_ref, x_ref, w_ref, hot_ref, out_ref, left_ref, prod_ref, acc_ref):
    acc_ref[...] = jnp.zeros_like(acc_ref)
    sign = jnp.where(lax.broadcasted_iota(jnp.int32, (8, 128), 0) < 4, -1.0, 1.0).astype(F32)

    def times_i(x):
        return sign * pltpu.roll(x, 4, 0)

    def pair(step, carry):
        row0 = pl.multiple_of(16 * step, 16)
        for pe in range(8):
            for h in range(2):
                src = pe * 8 + h * 4
                tiles = turn_blocks([x_ref[src + n, pl.ds(row0, 16), :] for n in range(4)])
                tiles = [t.astype(F32) for t in tiles]
                for ch in range(2):
                    for mm in range(2):
                        both = jnp.concatenate(
                            [tiles[2 * mm][8 * ch : 8 * ch + 8], tiles[2 * mm + 1][8 * ch : 8 * ch + 8]], axis=0
                        )
                        left_ref[ch, pe * 32 + mm * 16 : pe * 32 + mm * 16 + 16, 128 * h : 128 * h + 128] = both.astype(BF16)
        for ch in range(2):
            i = 2 * step + ch
            prod_ref[ch] = lax.dot_general(left_ref[ch], w_ref[i], NN, preferred_element_type=F32)
        for ch in range(2):
            i = 2 * step + ch
            sub = sub_ref[i]
            re = [[east_ref[i, s * 4 + e] for e in range(4)] for s in range(4)]
            im = [[east_ref[i, 16 + s * 4 + e] for e in range(4)] for s in range(4)]

            def frame_block(m4, carry):
                for h in range(2):
                    power = [None] * 4
                    for p in range(2):
                        y, iy = [], []
                        for e in range(4):
                            rows = pl.ds(pl.multiple_of((p * 4 + e) * 32 + m4 * 8, 8), 8)
                            both = prod_ref[ch, rows, 128 * h : 128 * h + 128] + times_i(
                                prod_ref[ch, rows, 256 + 128 * h : 384 + 128 * h]
                            )
                            y.append(both)
                            iy.append(times_i(both))
                        for s in range(4):
                            beam = y[0]
                            for e in range(1, 4):
                                if s == 0:
                                    beam = beam + y[e]
                                else:
                                    beam = beam + re[s][e] * y[e] + im[s][e] * iy[e]
                            square = beam * beam
                            power[s] = square if p == 0 else power[s] + square
                    for s in range(4):
                        cols = slice(s * 256 + h * 128, s * 256 + h * 128 + 128)
                        acc_ref[sub, m4, :, cols] += power[s]
                return carry

            lax.fori_loop(0, 4, frame_block, 0)
        return carry

    lax.fori_loop(0, 8, pair, 0)
    total = acc_ref[...].reshape(128, 1024)
    low_half = lax.broadcasted_iota(jnp.int32, (128, 1024), 0) % 8 < 4
    turned = acc_ref[...].reshape(16, 8, 1024)
    turned = jnp.concatenate([turned[:, 4:8], turned[:, 0:4]], axis=1).reshape(128, 1024)
    total = total + turned
    top = total.astype(BF16)
    rest = (total - top.astype(F32)).astype(BF16)
    parts = jnp.where(low_half, top, rest)
    out_ref[...] = lax.dot_general(hot_ref[...], parts, NT, preferred_element_type=F32).astype(BF16)


def beams(turned, east, subs, weights, hot):
    vmem, smem = pl.BlockSpec(memory_space=pltpu.VMEM), pl.BlockSpec(memory_space=pltpu.SMEM)
    return pl.pallas_call(
        beam_kernel,
        out_shape=jax.ShapeDtypeStruct((1024, 128), BF16),
        in_specs=[smem, smem, vmem, vmem, vmem],
        out_specs=vmem,
        scratch_shapes=[
            pltpu.VMEM((2, 256, 256), BF16),
            pltpu.VMEM((2, 256, 512), F32),
            pltpu.VMEM((4, 4, 8, 1024), F32),
        ],
        cost_estimate=pl.CostEstimate(
            flops=2_000_000_000, bytes_accessed=9_000_000, transcendentals=0
        ),
    )(east, subs, turned, weights, hot)


def beam_weights(channels):
    scale = 2 * C
    steps = scale - channels
    north = jnp.arange(256, dtype=jnp.int32)
    turns = steps[:, None, None] * (north[:, None] * north[None, :])[None] % (scale * 256)
    phases = (2.0 * math.pi / (scale * 256)) * turns.astype(F32)
    norm = 1.0 / math.sqrt(FEEDS)
    weights = jnp.concatenate([jnp.cos(phases), jnp.sin(phases)], axis=2) * norm
    four = jnp.arange(4, dtype=jnp.int32)
    turns = steps[:, None] * (four[:, None] * four[None, :]).reshape(1, 16) % (scale * 4)
    phases = (2.0 * math.pi / (scale * 4)) * turns.astype(F32)
    return weights.astype(BF16), jnp.concatenate([jnp.cos(phases), jnp.sin(phases)], axis=1)


def frame_tables():
    table = np.zeros((4, 4, 4, 2, 4, 4, 64), np.float32)
    for block in range(4):
        for m4 in range(4):
            for mb in range(4):
                row = np.full(64, -1.0 / 64.0)
                row[16 * block + 4 * mb + m4] += 1.0
                for sub in range(4):
                    table[block, sub, m4, :, mb, sub, :] = row / math.sqrt(C)
    return table.reshape(4, 128, 256).astype(jnp.bfloat16)


def three_parts(x):
    top = x.astype(BF16)
    rest = x - top.astype(F32)
    mid = rest.astype(BF16)
    return top, mid, (rest - mid.astype(F32)).astype(BF16)


def series_kernel(band_ref, s0_ref, s1_ref, s2_ref, s3_ref, tab_ref, delay_ref, out_ref, hot_ref, left_ref):
    series = None
    for back, ref in enumerate((s0_ref, s1_ref, s2_ref, s3_ref)):
        table = tab_ref[(4 - back) % 4]
        for part in three_parts(ref[...]):
            term = lax.dot_general(part, table, NN, preferred_element_type=F32)
            series = term if series is None else series + term
    back_shift = lax.broadcasted_iota(jnp.int32, (64, 128), 0)
    for s in range(16):
        hit = (back_shift + delay_ref[s : s + 1, :]) % 64 == 0
        hot_ref[64 * s : 64 * s + 64, :] = jnp.where(hit, 1.0, 0.0).astype(BF16)
    lane = lax.broadcasted_iota(jnp.int32, (16, 128), 1) % 64
    first = band_ref[0] * 16
    blocks = [series[16 * (at // 2) : 16 * (at // 2) + 16, 128 * (at % 2) : 128 * (at % 2) + 128] for at in range(8)]
    for t in range(64):
        for at in range(8):
            x = blocks[at]
            if t:
                x = jnp.where(lane < 64 - t, pltpu.roll(x, 128 - t, 1), pltpu.roll(x, 64 - t, 1))
            top = x.astype(BF16)
            left_ref[0, 16 * t : 16 * t + 16, 128 * at : 128 * at + 128] = top
            left_ref[1, 16 * t : 16 * t + 16, 128 * at : 128 * at + 128] = (x - top.astype(F32)).astype(BF16)

    def frames(step, carry):
        rows = pl.ds(pl.multiple_of(256 * step, 256), 256)
        hot = hot_ref[...]
        out = lax.dot_general(left_ref[0, rows, :], hot, NN, preferred_element_type=F32)
        out = out + lax.dot_general(left_ref[1, rows, :], hot, NN, preferred_element_type=F32)
        at = (first + 16 * step) % 64
        out_ref[pl.ds(at, 16)] = out.reshape(16, 16, 128)
        return carry

    lax.fori_loop(0, 4, frames, 0)


def series(band_at, sums, delays):
    vmem, smem = pl.BlockSpec(memory_space=pltpu.VMEM), pl.BlockSpec(memory_space=pltpu.SMEM)
    return pl.pallas_call(
        series_kernel,
        out_shape=jax.ShapeDtypeStruct((64, 16, 128), F32),
        in_specs=[smem] + [vmem] * 6,
        out_specs=vmem,
        scratch_shapes=[pltpu.VMEM((1024, 128), BF16), pltpu.VMEM((2, 1024, 1024), BF16)],
        cost_estimate=pl.CostEstimate(
            flops=600_000_000, bytes_accessed=1_000_000, transcendentals=0
        ),
    )(band_at.reshape(1), *sums, jnp.asarray(frame_tables()), delays)


def from_band(block, back):
    count = lax.axis_size("band")
    return lax.ppermute(block, "band", [(i, (i + back) % count) for i in range(count)])


def local(voltages, steering, chan_sub, delays):
    band_count = lax.axis_size("band")
    grp_at = lax.axis_index("grp")
    band_at = lax.axis_index("band")
    local_frames = voltages.shape[0]
    halo = lax.ppermute(
        voltages[local_frames - 3 :], "band", [(i, i + 1) for i in range(band_count - 1)]
    )
    turned_delays = jnp.transpose(delays)
    small = []
    for back in range(band_count):
        trials = lax.dynamic_slice_in_dim(
            turned_delays, (band_at + back) % band_count * 128, 128, axis=1
        )
        note = jnp.concatenate([chan_sub.reshape(2, 128), jnp.zeros((2, 128), jnp.int32), trials])
        small.append(note if back == 0 else from_band(note, back))
    quarter_at = grp_at // 16
    residue = grp_at % 16

    def owned_by(owner):
        found = small[0] * 0
        for back in range(band_count):
            found = found + jnp.where((band_at - back) % band_count == owner, small[back], 0)
        return found

    quarter_subs = owned_by(quarter_at)[0:2].reshape(16, 16)
    subs = lax.dynamic_slice_in_dim(quarter_subs, residue, 1, axis=1).reshape(16) % 4
    all_delays = jnp.concatenate([owned_by(owner)[4:8] for owner in range(band_count)])

    chunks = spectra(voltages, halo).reshape(64, 128, 128)
    turned = lax.all_to_all(chunks, "grp", split_axis=0, concat_axis=0, tiled=True)

    channels = quarter_at * 256 + 16 * jnp.arange(16, dtype=jnp.int32) + residue
    weights, east = beam_weights(channels)
    grid_at = steering[1] * 256 + steering[0]
    hot = (grid_at[:, None] == jnp.arange(1024, dtype=jnp.int32)[None, :]).astype(BF16)
    sums = beams(turned, east, subs, weights, hot).reshape(64, 16, 128)
    owned = lax.all_to_all(sums, "grp", split_axis=0, concat_axis=0, tiled=True)
    own = jnp.sum(owned.reshape(4, 16, 16, 128).astype(F32), axis=1).reshape(64, 128)
    every = [own if back == 0 else from_band(own, back) for back in range(band_count)]
    return series(band_at, every, all_delays)


def solution(mesh):
    in_specs = (P("band", "grp", None), P(), P("band"), P(None, "band"))
    out_specs = P(None, "grp", "band")
    return jax.shard_map(local, mesh=mesh, in_specs=in_specs, out_specs=out_specs, check_vma=False)
```

```python
import math

import jax
import jax.numpy as jnp
import numpy as np
from jax import lax
from jax.experimental import pallas as pl
from jax.experimental.pallas import tpu as pltpu
from jax.sharding import PartitionSpec as P

A = 2048
FEEDS = 1024
C = 1024
SAMP = 2048
BEAMS = 1024
TRIALS = 512
F32 = jnp.float32
BF16 = jnp.bfloat16
NT = (((1,), (1,)), ((), ()))
NN = (((1,), (0,)), ((), ()))


def window_taps():
    tap_pos = np.arange(4 * SAMP) + 0.5
    taper = 0.5 - 0.5 * np.cos(2.0 * np.pi / (4 * SAMP) * tap_pos)
    window = taper * np.sinc((tap_pos - 2 * SAMP) / SAMP)
    window = window * np.sqrt(SAMP / np.sum(window * window))
    return window.reshape(4, SAMP).astype(np.float32)


def lane_tables():
    k = np.arange(64)[:, None]
    lane = np.arange(128)[None, :]

    def rows(r, part):
        angle = 2.0 * np.pi / SAMP * (((16 * k + r) * lane) % SAMP)
        cos, sin = np.cos(angle) / np.sqrt(SAMP), np.sin(angle) / np.sqrt(SAMP)
        if part is not None:
            none = np.zeros_like(cos)
            pair = lambda x: np.concatenate([x, none] if part == 0 else [none, x], axis=1)
            return np.concatenate([pair(cos), pair(-sin)], axis=0)
        sign = -1.0 if r > 8 else 1.0
        top = np.concatenate([cos, -sin * sign], axis=1)
        return np.concatenate([top, np.concatenate([-sin, -cos * sign], axis=1)], axis=0)

    tables = [np.concatenate([rows(0, 0), rows(8, 1)], axis=0)]
    tables += [np.concatenate([rows(at, None), rows(16 - at, None)], axis=0) for at in range(1, 8)]
    return np.stack(tables).astype(jnp.bfloat16)


def real_dft16(x):
    h, c1, c3 = math.sqrt(0.5), math.cos(math.pi / 8), math.cos(3 * math.pi / 8)
    s = [x[j] + x[j + 8] for j in range(8)]
    d = [x[j] - x[j + 8] for j in range(8)]
    ss = [s[j] + s[j + 4] for j in range(4)]
    sd = [s[j] - s[j + 4] for j in range(4)]
    t0, t1 = ss[0] + ss[2], ss[1] + ss[3]
    out = [None] * 9
    out[0] = (t0 + t1, None)
    out[8] = (t0 - t1, None)
    out[4] = (ss[0] - ss[2], ss[1] - ss[3])
    dif, tot = h * (sd[1] - sd[3]), h * (sd[1] + sd[3])
    out[2] = (sd[0] + dif, sd[2] + tot)
    out[6] = (sd[0] - dif, tot - sd[2])
    p = [None] + [d[j] - d[8 - j] for j in (1, 2, 3)]
    q = [None] + [d[j] + d[8 - j] for j in (1, 2, 3)]
    hp, hq = h * p[2], h * q[2]
    ea, eb = d[0] + hp, d[0] - hp
    u, v = c1 * p[1] + c3 * p[3], c3 * p[1] - c1 * p[3]
    fa, fb = d[4] + hq, hq - d[4]
    y, z = c3 * q[1] + c1 * q[3], c1 * q[1] - c3 * q[3]
    out[1] = (ea + u, y + fa)
    out[7] = (ea - u, y - fa)
    out[3] = (eb + v, z + fb)
    out[5] = (eb - v, z - fb)
    return out


def frame_bins(part_ref, win_ref, row0, a0, frame, keep=None):
    lanes = []
    for jb in range(16):
        cols = slice(128 * jb, 128 * jb + 128)
        total = None
        for p in range(4):
            term = frame(p)[pl.ds(a0, 16), cols].astype(F32) * win_ref[p : p + 1, cols]
            if p == 3 and keep is not None:
                total = total * keep
            total = term if total is None else total + term
        lanes.append(total)
    rows = pl.ds(row0, 16)
    for at, (re, im) in enumerate(real_dft16(lanes)):
        if at % 8 == 0:
            part_ref[0, rows, 16 * at : 16 * at + 128] = re.astype(BF16)
        else:
            part_ref[at, rows, 0:128] = re.astype(BF16)
            part_ref[at, rows, 128:256] = im.astype(BF16)


def inner_kernel(v_ref, win_ref, part_ref):
    def body(step, carry):
        m = step // 2
        a0 = pl.multiple_of(16 * (step % 2), 16)
        frame_bins(part_ref, win_ref, pl.multiple_of(16 * step, 16), a0, lambda p: v_ref.at[m - 2 + p])
        return carry

    lax.fori_loop(4, 30, body, 0)


def spectra_kernel(
    band_ref, part_hbm, v_ref, prev_ref, next_ref, win_ref, tab_ref, out_ref, part_ref, turn_ref, sem
):
    inner = pl.ds(64, 416)
    fetch = pltpu.make_async_copy(part_hbm.at[:, inner, :], part_ref.at[:, inner, :], sem)
    fetch.start()
    keep = jnp.where(band_ref[0] == 3, 0.0, 1.0).astype(F32)

    def edge(half, carry):
        a0 = pl.multiple_of(16 * half, 16)
        for m in (0, 1):
            frame = lambda p, m=m: prev_ref.at[m + p] if m + p < 2 else v_ref.at[m + p - 2]
            frame_bins(part_ref, win_ref, pl.multiple_of(32 * m + a0, 16), a0, frame)
        frame = lambda p: v_ref.at[13 + p] if p < 3 else next_ref.at[0]
        frame_bins(part_ref, win_ref, pl.multiple_of(480 + a0, 16), a0, frame, keep)
        return carry

    lax.fori_loop(0, 2, edge, 0)
    fetch.wait()

    def transform(at, carry):
        rows = lax.dot_general(tab_ref[at], part_ref[at], NT, preferred_element_type=F32)
        for which in range(2):
            for reim in range(2):
                for mb in range(4):
                    r0 = 128 * which + 64 * reim
                    turn_ref[which, pl.ds(reim * 4 + mb, 64, stride=8), :] = rows[
                        r0 : r0 + 64, 128 * mb : 128 * mb + 128
                    ]
        for which in range(2):
            r = at if which == 0 else jnp.where(at == 0, 8, 16 - at)
            for q in range(4):
                out_ref[r, q] = turn_ref[which, 128 * q : 128 * q + 128, :].astype(BF16)
        return carry

    lax.fori_loop(0, 8, transform, 0)


def spectra(voltages, band_at):
    band_count = lax.axis_size("band")
    ahead = lax.ppermute(voltages[14:16], "band", [(i, i + 1) for i in range(band_count - 1)])
    behind = lax.ppermute(voltages[0:1], "band", [(i, (i - 1) % band_count) for i in range(band_count)])
    window, tables = jnp.asarray(window_taps()), jnp.asarray(lane_tables())
    vmem, smem = pl.BlockSpec(memory_space=pltpu.VMEM), pl.BlockSpec(memory_space=pltpu.SMEM)
    parts = pl.pallas_call(
        inner_kernel,
        name="inner_frames",
        out_shape=jax.ShapeDtypeStruct((8, 512, 256), BF16),
        in_specs=[vmem] * 2,
        out_specs=vmem,
        cost_estimate=pl.CostEstimate(flops=20_000_000, bytes_accessed=4_000_000, transcendentals=0),
    )(voltages, window)
    return pl.pallas_call(
        spectra_kernel,
        name="spectra",
        out_shape=jax.ShapeDtypeStruct((16, 4, 128, 128), BF16),
        in_specs=[smem, pl.BlockSpec(memory_space=pl.ANY)] + [vmem] * 5,
        out_specs=vmem,
        scratch_shapes=[
            pltpu.VMEM((8, 512, 256), BF16),
            pltpu.VMEM((2, 512, 128), F32),
            pltpu.SemaphoreType.DMA,
        ],
        cost_estimate=pl.CostEstimate(
            flops=600_000_000, bytes_accessed=6_000_000, transcendentals=0
        ),
    )(band_at.reshape(1), parts, voltages, ahead, behind, window, tables)


def turn_blocks(tiles):
    lane = lax.broadcasted_iota(jnp.int32, tiles[0].shape, 1)
    odd, high = (lane // 32) % 2 == 1, lane // 64 == 1
    one = [None] * 4
    for a, b in ((0, 1), (2, 3)):
        one[a] = jnp.where(odd, pltpu.roll(tiles[b], 32, 1), tiles[a])
        one[b] = jnp.where(odd, tiles[b], pltpu.roll(tiles[a], 96, 1))
    two = [None] * 4
    for a, b in ((0, 2), (1, 3)):
        two[a] = jnp.where(high, pltpu.roll(one[b], 64, 1), one[a])
        two[b] = jnp.where(high, one[b], pltpu.roll(one[a], 64, 1))
    return two


def beam_kernel(
    east_ref, sub_ref, x_ref, w_ref, hot_hbm, out_ref, left_ref, prod_ref, acc_ref, hot_ref, sem
):
    step = pl.program_id(0)
    fetch = pltpu.make_async_copy(hot_hbm, hot_ref, sem)

    @pl.when(step == 0)
    def _():
        fetch.start()
        acc_ref[...] = jnp.zeros_like(acc_ref)

    low = lax.broadcasted_iota(jnp.int32, (8, 128), 0) < 4
    row0 = pl.multiple_of(16 * step, 16)
    for pe in range(8):
        for h in range(2):
            src = pe * 8 + h * 4
            tiles = turn_blocks([x_ref[src + n, pl.ds(row0, 16), :] for n in range(4)])
            tiles = [t.astype(F32) for t in tiles]
            for ch in range(2):
                one = [t[8 * ch : 8 * ch + 8] for t in tiles]
                re = [jnp.where(low, one[a], pltpu.roll(one[a + 1], 4, 0)) for a in (0, 2)]
                im = [jnp.where(low, pltpu.roll(one[a], 4, 0), one[a + 1]) for a in (0, 2)]
                re, im = jnp.concatenate(re, axis=0), jnp.concatenate(im, axis=0)
                rows, cols = slice(16 * pe, 16 * pe + 16), slice(128 * h, 128 * h + 128)
                more = slice(256 + 128 * h, 384 + 128 * h)
                left_ref[ch, 0, rows, cols] = re.astype(BF16)
                left_ref[ch, 0, rows, more] = (-im).astype(BF16)
                left_ref[ch, 1, rows, cols] = re.astype(BF16)
                left_ref[ch, 1, rows, more] = im.astype(BF16)
    for ch in range(2):
        for part in range(2):
            prod_ref[ch, part] = lax.dot_general(
                left_ref[ch, part], w_ref[ch, 256 * part : 256 * part + 512, :], NN, preferred_element_type=F32
            )
    for ch in range(2):
        i = 2 * step + ch
        sub = sub_ref[i]
        cos = [[east_ref[i, s * 4 + e] for e in range(4)] for s in range(4)]
        sin = [[east_ref[i, 16 + s * 4 + e] for e in range(4)] for s in range(4)]
        for t in range(2):
            for h in range(2):
                power = [None] * 4
                for p in range(2):
                    re, im = [], []
                    for e in range(4):
                        r0 = p * 64 + e * 16 + t * 8
                        re.append(prod_ref[ch, 0, r0 : r0 + 8, 128 * h : 128 * h + 128])
                        im.append(prod_ref[ch, 1, r0 : r0 + 8, 128 * h : 128 * h + 128])
                    for s in range(4):
                        beam_re, beam_im = re[0], im[0]
                        for e in range(1, 4):
                            if s == 0:
                                beam_re, beam_im = beam_re + re[e], beam_im + im[e]
                            else:
                                c, d = cos[s][e], sin[s][e]
                                beam_re = beam_re + (c * re[e] - d * im[e])
                                beam_im = beam_im + (c * im[e] + d * re[e])
                        square = beam_re * beam_re + beam_im * beam_im
                        power[s] = square if p == 0 else power[s] + square
                for s in range(4):
                    cols = slice(s * 256 + h * 128, s * 256 + h * 128 + 128)
                    acc_ref[sub, 8 * t : 8 * t + 8, cols] += power[s]

    @pl.when(step == pl.num_programs(0) - 1)
    def _():
        total = acc_ref[...].reshape(64, 1024)
        top = total.astype(BF16)
        rest = (total - top.astype(F32)).astype(BF16)
        parts = jnp.concatenate([top, rest], axis=0)
        fetch.wait()
        out_ref[...] = lax.dot_general(hot_ref[...], parts, NT, preferred_element_type=F32).astype(BF16)


def beams(turned, east, subs, weights, hot):
    smem = pl.BlockSpec(memory_space=pltpu.SMEM)
    return pl.pallas_call(
        beam_kernel,
        name="beams",
        grid=(8,),
        out_shape=jax.ShapeDtypeStruct((1024, 128), BF16),
        in_specs=[
            smem,
            smem,
            pl.BlockSpec((64, 128, 128), lambda i: (0, 0, 0)),
            pl.BlockSpec((2, 768, 256), lambda i: (i, 0, 0)),
            pl.BlockSpec(memory_space=pl.ANY),
        ],
        out_specs=pl.BlockSpec((1024, 128), lambda i: (0, 0)),
        scratch_shapes=[
            pltpu.VMEM((2, 2, 128, 512), BF16),
            pltpu.VMEM((2, 2, 128, 256), F32),
            pltpu.VMEM((4, 16, 1024), F32),
            pltpu.VMEM((1024, 1024), BF16),
            pltpu.SemaphoreType.DMA,
        ],
        cost_estimate=pl.CostEstimate(
            flops=2_000_000_000, bytes_accessed=11_000_000, transcendentals=0
        ),
    )(east, subs, turned, weights, hot)


def beam_weights(channels):
    scale = 2 * C
    steps = scale - channels
    north = jnp.arange(256, dtype=jnp.int32)
    turns = steps[:, None, None] * (north[:, None] * north[None, :])[None] % (scale * 256)
    phases = (2.0 * math.pi / (scale * 256)) * turns.astype(F32)
    norm = 1.0 / math.sqrt(FEEDS)
    cos, sin = (jnp.cos(phases) * norm).astype(BF16), (jnp.sin(phases) * norm).astype(BF16)
    four = jnp.arange(4, dtype=jnp.int32)
    turns = steps[:, None] * (four[:, None] * four[None, :]).reshape(1, 16) % (scale * 4)
    phases = (2.0 * math.pi / (scale * 4)) * turns.astype(F32)
    return jnp.concatenate([cos, sin, cos], axis=1), jnp.concatenate([jnp.cos(phases), jnp.sin(phases)], axis=1)


def gather_kernel(x_ref, out_ref):
    total = x_ref[0].astype(F32)
    for r in range(1, 16):
        total = total + x_ref[r].astype(F32)
    total = total + pltpu.roll(total, 64, 1)
    top = total.astype(BF16)
    rest = (total - top.astype(F32)).astype(BF16)
    lane = lax.broadcasted_iota(jnp.int32, (64, 128), 1)
    both = jnp.where(lane < 64, top, rest)
    for q in range(4):
        for band in range(4):
            out_ref[4 * q + band] = both[16 * q : 16 * q + 16, :]


def gather_residues(pieces):
    vmem = pl.BlockSpec(memory_space=pltpu.VMEM)
    return pl.pallas_call(
        gather_kernel,
        name="residues",
        out_shape=jax.ShapeDtypeStruct((16, 16, 128), BF16),
        in_specs=[vmem],
        out_specs=vmem,
    )(pieces)


def frame_tables():
    table = np.zeros((4, 2, 4, 4, 4, 4, 64), np.float32)
    for band in range(4):
        for m4 in range(4):
            for mb in range(4):
                row = np.full(64, -1.0 / 64.0)
                row[(16 * band + 1 + 4 * mb + m4) % 64] += 1.0
                for sub in range(4):
                    table[band, :, sub, m4, mb, sub, :] = row / math.sqrt(C)
    return table.reshape(4, 128, 256).astype(jnp.bfloat16)


def series_kernel(x_ref, tab_ref, delay_ref, out_ref, hot_ref, left_ref):
    series = None
    for band in range(4):
        rows = jnp.concatenate([x_ref[4 * q + band] for q in range(4)], axis=0)
        term = lax.dot_general(rows, tab_ref[band], NN, preferred_element_type=F32)
        series = term if series is None else series + term
    ahead = lax.broadcasted_iota(jnp.int32, (64, 128), 0)
    for s in range(16):
        hit = (ahead + delay_ref[s : s + 1, :]) % 64 == 0
        hot = jnp.where(hit, 1.0, 0.0).astype(BF16)
        for th in range(4):
            cols = slice(128 * th, 128 * th + 128)
            for tile in range(4):
                to = 64 * s + 16 * tile
                at = 16 * ((tile - th) % 4)
                hot_ref[to : to + 16, cols] = hot[at : at + 16, :]
    lane = lax.broadcasted_iota(jnp.int32, (16, 128), 1) % 64
    for at in range(8):
        rows, cols = slice(16 * (at // 2), 16 * (at // 2) + 16), slice(128 * (at % 2), 128 * (at % 2) + 128)
        block = series[rows, cols]
        for t in range(16):
            x = block
            if t:
                x = jnp.where(lane < 64 - t, pltpu.roll(x, 128 - t, 1), pltpu.roll(x, 64 - t, 1))
            top = x.astype(BF16)
            left_ref[0, 16 * t : 16 * t + 16, 128 * at : 128 * at + 128] = top
            left_ref[1, 16 * t : 16 * t + 16, 128 * at : 128 * at + 128] = (x - top.astype(F32)).astype(BF16)
    hot = hot_ref[...]
    out = lax.dot_general(left_ref[0], hot, NN, preferred_element_type=F32)
    out = out + lax.dot_general(left_ref[1], hot, NN, preferred_element_type=F32)
    for th in range(4):
        out_ref[16 * th : 16 * th + 16] = out[:, 128 * th : 128 * th + 128].reshape(16, 16, 128)


def series(sums, delays):
    vmem = pl.BlockSpec(memory_space=pltpu.VMEM)
    return pl.pallas_call(
        series_kernel,
        name="series",
        out_shape=jax.ShapeDtypeStruct((64, 16, 128), F32),
        in_specs=[vmem] * 3,
        out_specs=vmem,
        scratch_shapes=[pltpu.VMEM((1024, 512), BF16), pltpu.VMEM((2, 256, 1024), BF16)],
        cost_estimate=pl.CostEstimate(
            flops=600_000_000, bytes_accessed=1_000_000, transcendentals=0
        ),
    )(sums, jnp.asarray(frame_tables()), delays)


def from_band(block, back):
    count = lax.axis_size("band")
    return lax.ppermute(block, "band", [(i, (i + back) % count) for i in range(count)])


def local(voltages, steering, chan_sub, delays):
    groups, band_count = lax.axis_size("grp"), lax.axis_size("band")
    grp_at = lax.axis_index("grp")
    band_at = lax.axis_index("band")
    turned_delays = jnp.transpose(delays)
    small = []
    for back in range(band_count):
        trials = lax.dynamic_slice_in_dim(
            turned_delays, (band_at + back) % band_count * 128, 128, axis=1
        )
        note = jnp.concatenate([chan_sub.reshape(2, 128), jnp.zeros((2, 128), jnp.int32), trials])
        small.append(note if back == 0 else from_band(note, back))
    quarter_at = grp_at % 4
    residue = grp_at // 4

    def owned_by(owner):
        found = small[0] * 0
        for back in range(band_count):
            found = found + jnp.where((band_at - back) % band_count == owner, small[back], 0)
        return found

    quarter_subs = owned_by(quarter_at)[0:2].reshape(16, 16)
    subs = lax.dynamic_slice_in_dim(quarter_subs, residue, 1, axis=1).reshape(16) % 4
    all_delays = jnp.concatenate([owned_by(owner)[4:8] for owner in range(band_count)])

    chunks = spectra(voltages, band_at).reshape(64, 128, 128)
    turned = lax.all_to_all(chunks, "grp", split_axis=0, concat_axis=0, tiled=True)

    channels = quarter_at * 256 + 16 * jnp.arange(16, dtype=jnp.int32) + residue
    weights, east = beam_weights(channels)
    grid_at = steering[1] * 256 + steering[0]
    hot = (grid_at[:, None] == jnp.arange(1024, dtype=jnp.int32)[None, :]).astype(BF16)
    sums = beams(turned, east, subs, weights, hot).reshape(16, 64, 128)
    planes = [[4 * r + q for r in range(groups // 4)] for q in range(4)]
    pieces = lax.all_to_all(
        sums, "grp", split_axis=0, concat_axis=0, tiled=True, axis_index_groups=planes
    )
    columns = [
        [(4 * r + q) * band_count + band for q in range(4) for band in range(band_count)]
        for r in range(groups // 4)
    ]
    every = lax.all_to_all(
        gather_residues(pieces),
        ("grp", "band"),
        split_axis=0,
        concat_axis=0,
        tiled=True,
        axis_index_groups=columns,
    )
    return series(every, all_delays)


def solution(mesh):
    in_specs = (P("band", "grp", None), P(), P("band"), P(None, "band"))
    out_specs = P(None, "grp", "band")
    return jax.shard_map(local, mesh=mesh, in_specs=in_specs, out_specs=out_specs, check_vma=False)
```

```python
import math

import jax
import jax.numpy as jnp
import numpy as np
from jax import lax
from jax.experimental import pallas as pl
from jax.experimental.pallas import tpu as pltpu
from jax.sharding import PartitionSpec as P

A = 2048
FEEDS = 1024
C = 1024
SAMP = 2048
BEAMS = 1024
TRIALS = 512
F32 = jnp.float32
BF16 = jnp.bfloat16
MIB = 1 << 20
NT = (((1,), (1,)), ((), ()))
NN = (((1,), (0,)), ((), ()))


def window_taps():
    tap_pos = np.arange(4 * SAMP) + 0.5
    taper = 0.5 - 0.5 * np.cos(2.0 * np.pi / (4 * SAMP) * tap_pos)
    window = taper * np.sinc((tap_pos - 2 * SAMP) / SAMP)
    window = window * np.sqrt(SAMP / np.sum(window * window))
    return window.reshape(4, SAMP).astype(np.float32)


def lane_tables():
    k = np.arange(64)[:, None]
    lane = np.arange(128)[None, :]

    def rows(r, part):
        angle = 2.0 * np.pi / SAMP * (((16 * k + r) * lane) % SAMP)
        cos, sin = np.cos(angle) / np.sqrt(SAMP), np.sin(angle) / np.sqrt(SAMP)
        if part is not None:
            none = np.zeros_like(cos)
            pair = lambda x: np.concatenate([x, none] if part == 0 else [none, x], axis=1)
            return np.concatenate([pair(cos), pair(-sin)], axis=0)
        sign = -1.0 if r > 8 else 1.0
        top = np.concatenate([cos, -sin * sign], axis=1)
        return np.concatenate([top, np.concatenate([-sin, -cos * sign], axis=1)], axis=0)

    tables = [np.concatenate([rows(0, 0), rows(8, 1)], axis=0)]
    tables += [np.concatenate([rows(at, None), rows(16 - at, None)], axis=0) for at in range(1, 8)]
    return np.stack(tables).astype(jnp.bfloat16)


def real_dft16(x):
    h, c1, c3 = math.sqrt(0.5), math.cos(math.pi / 8), math.cos(3 * math.pi / 8)
    s = [x[j] + x[j + 8] for j in range(8)]
    d = [x[j] - x[j + 8] for j in range(8)]
    ss = [s[j] + s[j + 4] for j in range(4)]
    sd = [s[j] - s[j + 4] for j in range(4)]
    t0, t1 = ss[0] + ss[2], ss[1] + ss[3]
    out = [None] * 9
    out[0] = (t0 + t1, None)
    out[8] = (t0 - t1, None)
    out[4] = (ss[0] - ss[2], ss[1] - ss[3])
    dif, tot = h * (sd[1] - sd[3]), h * (sd[1] + sd[3])
    out[2] = (sd[0] + dif, sd[2] + tot)
    out[6] = (sd[0] - dif, tot - sd[2])
    p = [None] + [d[j] - d[8 - j] for j in (1, 2, 3)]
    q = [None] + [d[j] + d[8 - j] for j in (1, 2, 3)]
    hp, hq = h * p[2], h * q[2]
    ea, eb = d[0] + hp, d[0] - hp
    u, v = c1 * p[1] + c3 * p[3], c3 * p[1] - c1 * p[3]
    fa, fb = d[4] + hq, hq - d[4]
    y, z = c3 * q[1] + c1 * q[3], c1 * q[1] - c3 * q[3]
    out[1] = (ea + u, y + fa)
    out[7] = (ea - u, y - fa)
    out[3] = (eb + v, z + fb)
    out[5] = (eb - v, z - fb)
    return out


def frame_bins(part_ref, win_ref, row0, a0, frame, keep=None):
    lanes = []
    for jb in range(16):
        cols = slice(128 * jb, 128 * jb + 128)
        total = None
        for p in range(4):
            term = frame(p)[pl.ds(a0, 16), cols].astype(F32) * win_ref[p : p + 1, cols]
            if p == 3 and keep is not None:
                total = total * keep
            total = term if total is None else total + term
        lanes.append(total)
    rows = pl.ds(row0, 16)
    for at, (re, im) in enumerate(real_dft16(lanes)):
        if at % 8 == 0:
            part_ref[0, rows, 16 * at : 16 * at + 128] = re.astype(BF16)
        else:
            part_ref[at, rows, 0:128] = re.astype(BF16)
            part_ref[at, rows, 128:256] = im.astype(BF16)


def inner_kernel(v_ref, win_ref, part_ref):
    def body(step, carry):
        m = step // 2
        a0 = pl.multiple_of(16 * (step % 2), 16)
        frame_bins(part_ref, win_ref, pl.multiple_of(16 * step, 16), a0, lambda p: v_ref.at[m - 2 + p])
        return carry

    lax.fori_loop(4, 30, body, 0)


def spectra_kernel(
    band_ref, part_hbm, v_hbm, prev_ref, next_ref, win_ref, tab_hbm, out_hbm,
    part_ref, edge_ref, tab_ref, stage_ref, turn_ref, in_sem, out_sem
):
    inner = pl.ds(64, 416)
    first = pltpu.make_async_copy(v_hbm.at[0:3], edge_ref.at[0:3], in_sem.at[0])
    last = pltpu.make_async_copy(v_hbm.at[13:16], edge_ref.at[3:6], in_sem.at[1])
    parts = pltpu.make_async_copy(part_hbm.at[:, inner, :], part_ref.at[:, inner, :], in_sem.at[2])
    tables = pltpu.make_async_copy(tab_hbm, tab_ref, in_sem.at[3])
    for copy in (first, last, parts, tables):
        copy.start()
    keep = jnp.where(band_ref[0] == 3, 0.0, 1.0).astype(F32)
    first.wait()
    last.wait()

    def edge(half, carry):
        a0 = pl.multiple_of(16 * half, 16)
        for m in (0, 1):
            frame = lambda p, m=m: prev_ref.at[m + p] if m + p < 2 else edge_ref.at[m + p - 2]
            frame_bins(part_ref, win_ref, pl.multiple_of(32 * m + a0, 16), a0, frame)
        frame = lambda p: edge_ref.at[3 + p] if p < 3 else next_ref.at[0]
        frame_bins(part_ref, win_ref, pl.multiple_of(480 + a0, 16), a0, frame, keep)
        return carry

    lax.fori_loop(0, 2, edge, 0)
    parts.wait()
    tables.wait()
    sent = []
    for at in range(8):
        rows = lax.dot_general(tab_ref[at], part_ref[at], NT, preferred_element_type=F32)
        for which in range(2):
            slot = 2 * (at % 2) + which
            for reim in range(2):
                for mb in range(4):
                    r0 = 128 * which + 64 * reim
                    turn_ref[slot, pl.ds(reim * 4 + mb, 64, stride=8), :] = rows[
                        r0 : r0 + 64, 128 * mb : 128 * mb + 128
                    ]
        for which in range(2):
            slot = 2 * (at % 2) + which
            r = at if which == 0 else (8 if at == 0 else 16 - at)
            for q in range(4):
                stage_ref[r, q] = turn_ref[slot, 128 * q : 128 * q + 128, :].astype(BF16)
            copy = pltpu.make_async_copy(stage_ref.at[r], out_hbm.at[r], out_sem.at[r])
            copy.start()
            sent.append(copy)
    for copy in sent:
        copy.wait()


def spectra(voltages, band_at):
    band_count = lax.axis_size("band")
    ahead = lax.ppermute(voltages[14:16], "band", [(i, i + 1) for i in range(band_count - 1)])
    behind = lax.ppermute(voltages[0:1], "band", [(i, (i - 1) % band_count) for i in range(band_count)])
    window, tables = jnp.asarray(window_taps()), jnp.asarray(lane_tables())
    vmem, smem = pl.BlockSpec(memory_space=pltpu.VMEM), pl.BlockSpec(memory_space=pltpu.SMEM)
    anywhere = pl.BlockSpec(memory_space=pl.ANY)
    parts = pl.pallas_call(
        inner_kernel,
        name="inner_frames",
        out_shape=jax.ShapeDtypeStruct((8, 512, 256), BF16),
        in_specs=[vmem] * 2,
        out_specs=vmem,
        compiler_params=pltpu.CompilerParams(vmem_limit_bytes=58 * MIB),
        cost_estimate=pl.CostEstimate(flops=20_000_000, bytes_accessed=4_000_000, transcendentals=0),
    )(voltages, window)
    return pl.pallas_call(
        spectra_kernel,
        name="spectra",
        out_shape=jax.ShapeDtypeStruct((16, 4, 128, 128), BF16),
        in_specs=[smem, anywhere, anywhere, vmem, vmem, vmem, anywhere],
        out_specs=pl.BlockSpec(memory_space=pltpu.HBM),
        scratch_shapes=[
            pltpu.VMEM((8, 512, 256), BF16),
            pltpu.VMEM((6, 32, 2048), BF16),
            pltpu.VMEM((8, 256, 256), BF16),
            pltpu.VMEM((16, 4, 128, 128), BF16),
            pltpu.VMEM((4, 512, 128), F32),
            pltpu.SemaphoreType.DMA((4,)),
            pltpu.SemaphoreType.DMA((16,)),
        ],
        compiler_params=pltpu.CompilerParams(vmem_limit_bytes=52 * MIB),
        cost_estimate=pl.CostEstimate(
            flops=600_000_000, bytes_accessed=6_000_000, transcendentals=0
        ),
    )(band_at.reshape(1), parts, voltages, ahead, behind, window, tables)


def turn_blocks(tiles):
    lane = lax.broadcasted_iota(jnp.int32, tiles[0].shape, 1)
    odd, high = (lane // 32) % 2 == 1, lane // 64 == 1
    one = [None] * 4
    for a, b in ((0, 1), (2, 3)):
        one[a] = jnp.where(odd, pltpu.roll(tiles[b], 32, 1), tiles[a])
        one[b] = jnp.where(odd, tiles[b], pltpu.roll(tiles[a], 96, 1))
    two = [None] * 4
    for a, b in ((0, 2), (1, 3)):
        two[a] = jnp.where(high, pltpu.roll(one[b], 64, 1), one[a])
        two[b] = jnp.where(high, one[b], pltpu.roll(one[a], 64, 1))
    return two


def place_channels(x_ref, left_ref):
    low = lax.broadcasted_iota(jnp.int32, (8, 128), 0) < 4
    for pe in range(8):
        for h in range(2):
            src = pe * 8 + h * 4
            tiles = turn_blocks([x_ref[src + n] for n in range(4)])
            tiles = [t.astype(F32) for t in tiles]
            for ch in range(2):
                one = [t[8 * ch : 8 * ch + 8] for t in tiles]
                re = [jnp.where(low, one[a], pltpu.roll(one[a + 1], 4, 0)) for a in (0, 2)]
                im = [jnp.where(low, pltpu.roll(one[a], 4, 0), one[a + 1]) for a in (0, 2)]
                re = jnp.concatenate(re, axis=0).astype(BF16)
                im = jnp.concatenate(im, axis=0).astype(BF16)
                rows, cols = slice(16 * pe, 16 * pe + 16), slice(128 * h, 128 * h + 128)
                more = slice(256 + 128 * h, 384 + 128 * h)
                left_ref[ch, 0, rows, cols] = re
                left_ref[ch, 0, rows, more] = -im
                left_ref[ch, 1, rows, cols] = re
                left_ref[ch, 1, rows, more] = im


def add_powers(pair, east_ref, sub_ref, prod_ref, acc_ref):
    for ch in range(2):
        i = 2 * pair + ch
        sub = sub_ref[i]
        cos = [[east_ref[i, s * 4 + e] for e in range(4)] for s in range(4)]
        sin = [[east_ref[i, 16 + s * 4 + e] for e in range(4)] for s in range(4)]
        for t in range(2):
            for h in range(2):
                power = [None] * 4
                for p in range(2):
                    re, im = [], []
                    for e in range(4):
                        r0 = p * 64 + e * 16 + t * 8
                        re.append(prod_ref[ch, 0, r0 : r0 + 8, 128 * h : 128 * h + 128])
                        im.append(prod_ref[ch, 1, r0 : r0 + 8, 128 * h : 128 * h + 128])
                    for s in range(4):
                        beam_re, beam_im = re[0], im[0]
                        for e in range(1, 4):
                            if s == 0:
                                beam_re, beam_im = beam_re + re[e], beam_im + im[e]
                            else:
                                c, d = cos[s][e], sin[s][e]
                                beam_re = beam_re + (c * re[e] - d * im[e])
                                beam_im = beam_im + (c * im[e] + d * re[e])
                        square = beam_re * beam_re + beam_im * beam_im
                        power[s] = square if p == 0 else power[s] + square
                for s in range(4):
                    cols = slice(s * 256 + h * 128, s * 256 + h * 128 + 128)
                    acc_ref[sub, 8 * t : 8 * t + 8, cols] += power[s]


def beam_kernel(
    east_ref, sub_ref, first_ref, next_ref, w_ref, hot_hbm, out_ref, left_ref, prod_ref, acc_ref, hot_ref, sem
):
    step = pl.program_id(0)
    fetch = pltpu.make_async_copy(hot_hbm, hot_ref, sem)

    @pl.when(step == 0)
    def _():
        fetch.start()
        acc_ref[...] = jnp.zeros_like(acc_ref)
        prod_ref[...] = jnp.zeros_like(prod_ref)
        place_channels(first_ref, left_ref)

    add_powers(jnp.maximum(step - 1, 0), east_ref, sub_ref, prod_ref, acc_ref)
    for ch in range(2):
        for part in range(2):
            prod_ref[ch, part] = lax.dot_general(
                left_ref[ch, part], w_ref[ch, 256 * part : 256 * part + 512, :], NN, preferred_element_type=F32
            )
    place_channels(next_ref, left_ref)

    @pl.when(step == pl.num_programs(0) - 1)
    def _():
        add_powers(step, east_ref, sub_ref, prod_ref, acc_ref)
        total = acc_ref[...].reshape(64, 1024)
        top = total.astype(BF16)
        rest = (total - top.astype(F32)).astype(BF16)
        parts = jnp.concatenate([top, rest], axis=0)
        fetch.wait()
        out_ref[...] = lax.dot_general(hot_ref[...], parts, NT, preferred_element_type=F32).astype(BF16)


def beams(turned, east, subs, weights, hot):
    smem = pl.BlockSpec(memory_space=pltpu.SMEM)
    return pl.pallas_call(
        beam_kernel,
        name="beams",
        grid=(8,),
        out_shape=jax.ShapeDtypeStruct((1024, 128), BF16),
        in_specs=[
            smem,
            smem,
            pl.BlockSpec((64, 16, 128), lambda i: (0, 0, 0)),
            pl.BlockSpec((64, 16, 128), lambda i: (0, jnp.minimum(i + 1, 7), 0)),
            pl.BlockSpec((2, 768, 256), lambda i: (i, 0, 0)),
            pl.BlockSpec(memory_space=pl.ANY),
        ],
        out_specs=pl.BlockSpec((1024, 128), lambda i: (0, 0)),
        scratch_shapes=[
            pltpu.VMEM((2, 2, 128, 512), BF16),
            pltpu.VMEM((2, 2, 128, 256), F32),
            pltpu.VMEM((4, 16, 1024), F32),
            pltpu.VMEM((1024, 1024), BF16),
            pltpu.SemaphoreType.DMA,
        ],
        compiler_params=pltpu.CompilerParams(vmem_limit_bytes=51 * MIB),
        cost_estimate=pl.CostEstimate(
            flops=2_000_000_000, bytes_accessed=11_000_000, transcendentals=0
        ),
    )(east, subs, turned, turned, weights, hot)


def weight_kernel(step_ref, out_ref):
    scale = 2 * C * 256
    row = lax.broadcasted_iota(jnp.int32, (16, 256), 0)
    north = lax.broadcasted_iota(jnp.int32, (16, 256), 1)
    for ch in range(2):
        rate = step_ref[2 * pl.program_id(0) + ch]

        def turn(feeds):
            phases = (2.0 * math.pi / scale) * ((rate * (feeds * north)) % scale).astype(F32)
            return jnp.cos(phases), jnp.sin(phases)

        norm = 1.0 / math.sqrt(FEEDS)
        cos, sin = turn(row)
        cos, sin = cos * norm, sin * norm
        more_cos, more_sin = turn(16 + 0 * row)
        for tile in range(16):
            if tile:
                cos, sin = cos * more_cos - sin * more_sin, sin * more_cos + cos * more_sin
            r0 = 16 * tile
            out_ref[ch, r0 : r0 + 16, :] = cos.astype(BF16)
            out_ref[ch, 256 + r0 : 272 + r0, :] = sin.astype(BF16)
            out_ref[ch, 512 + r0 : 528 + r0, :] = cos.astype(BF16)


def beam_weights(channels):
    scale = 2 * C
    steps = scale - channels
    weights = pl.pallas_call(
        weight_kernel,
        name="weights",
        grid=(8,),
        out_shape=jax.ShapeDtypeStruct((16, 768, 256), BF16),
        in_specs=[pl.BlockSpec(memory_space=pltpu.SMEM)],
        out_specs=pl.BlockSpec((2, 768, 256), lambda i: (i, 0, 0)),
        compiler_params=pltpu.CompilerParams(vmem_limit_bytes=56 * MIB),
        cost_estimate=pl.CostEstimate(flops=20_000_000, bytes_accessed=6_000_000, transcendentals=500_000),
    )(steps)
    four = jnp.arange(4, dtype=jnp.int32)
    turns = steps[:, None] * (four[:, None] * four[None, :]).reshape(1, 16) % (scale * 4)
    phases = (2.0 * math.pi / (scale * 4)) * turns.astype(F32)
    return weights, jnp.concatenate([jnp.cos(phases), jnp.sin(phases)], axis=1)


def gather_kernel(x_ref, out_ref):
    total = x_ref[0].astype(F32)
    for r in range(1, 16):
        total = total + x_ref[r].astype(F32)
    total = total + pltpu.roll(total, 64, 1)
    top = total.astype(BF16)
    rest = (total - top.astype(F32)).astype(BF16)
    lane = lax.broadcasted_iota(jnp.int32, (64, 128), 1)
    both = jnp.where(lane < 64, top, rest)
    for q in range(4):
        for band in range(4):
            out_ref[4 * q + band] = both[16 * q : 16 * q + 16, :]


def gather_residues(pieces):
    vmem = pl.BlockSpec(memory_space=pltpu.VMEM)
    return pl.pallas_call(
        gather_kernel,
        name="residues",
        out_shape=jax.ShapeDtypeStruct((16, 16, 128), BF16),
        in_specs=[vmem],
        out_specs=vmem,
        compiler_params=pltpu.CompilerParams(vmem_limit_bytes=4 * MIB),
    )(pieces)


def frame_tables():
    table = np.zeros((4, 2, 4, 4, 4, 4, 64), np.float32)
    for band in range(4):
        for m4 in range(4):
            for mb in range(4):
                row = np.full(64, -1.0 / 64.0)
                row[(16 * band + 1 + 4 * mb + m4) % 64] += 1.0
                for sub in range(4):
                    table[band, :, sub, m4, mb, sub, :] = row / math.sqrt(C)
    return table.reshape(4, 128, 256).astype(jnp.bfloat16)


def series_kernel(x_ref, tab_ref, delay_ref, out_ref, hot_ref, left_ref):
    series = None
    for band in range(4):
        rows = jnp.concatenate([x_ref[4 * q + band] for q in range(4)], axis=0)
        term = lax.dot_general(rows, tab_ref[band], NN, preferred_element_type=F32)
        series = term if series is None else series + term
    ahead = lax.broadcasted_iota(jnp.int32, (64, 128), 0)
    for s in range(16):
        hit = (ahead + delay_ref[s : s + 1, :]) % 64 == 0
        hot = jnp.where(hit, 1.0, 0.0).astype(BF16)
        for th in range(4):
            cols = slice(128 * th, 128 * th + 128)
            for tile in range(4):
                to = 64 * s + 16 * tile
                at = 16 * ((tile - th) % 4)
                hot_ref[to : to + 16, cols] = hot[at : at + 16, :]
    lane = lax.broadcasted_iota(jnp.int32, (16, 128), 1) % 64
    for at in range(8):
        rows, cols = slice(16 * (at // 2), 16 * (at // 2) + 16), slice(128 * (at % 2), 128 * (at % 2) + 128)
        block = series[rows, cols]
        for t in range(16):
            x = block
            if t:
                x = jnp.where(lane < 64 - t, pltpu.roll(x, 128 - t, 1), pltpu.roll(x, 64 - t, 1))
            top = x.astype(BF16)
            left_ref[0, 16 * t : 16 * t + 16, 128 * at : 128 * at + 128] = top
            left_ref[1, 16 * t : 16 * t + 16, 128 * at : 128 * at + 128] = (x - top.astype(F32)).astype(BF16)
    hot = hot_ref[...]
    out = lax.dot_general(left_ref[0], hot, NN, preferred_element_type=F32)
    out = out + lax.dot_general(left_ref[1], hot, NN, preferred_element_type=F32)
    for th in range(4):
        out_ref[16 * th : 16 * th + 16] = out[:, 128 * th : 128 * th + 128].reshape(16, 16, 128)


def series(sums, delays):
    vmem = pl.BlockSpec(memory_space=pltpu.VMEM)
    return pl.pallas_call(
        series_kernel,
        name="series",
        out_shape=jax.ShapeDtypeStruct((64, 16, 128), F32),
        in_specs=[vmem] * 3,
        out_specs=vmem,
        scratch_shapes=[pltpu.VMEM((1024, 512), BF16), pltpu.VMEM((2, 256, 1024), BF16)],
        compiler_params=pltpu.CompilerParams(vmem_limit_bytes=8 * MIB),
        cost_estimate=pl.CostEstimate(
            flops=600_000_000, bytes_accessed=1_000_000, transcendentals=0
        ),
    )(sums, jnp.asarray(frame_tables()), delays)


def from_band(block, back):
    count = lax.axis_size("band")
    return lax.ppermute(block, "band", [(i, (i + back) % count) for i in range(count)])


def local(voltages, steering, chan_sub, delays):
    groups, band_count = lax.axis_size("grp"), lax.axis_size("band")
    grp_at = lax.axis_index("grp")
    band_at = lax.axis_index("band")
    turned_delays = jnp.transpose(delays)
    small = []
    for back in range(band_count):
        trials = lax.dynamic_slice_in_dim(
            turned_delays, (band_at + back) % band_count * 128, 128, axis=1
        )
        note = jnp.concatenate([chan_sub.reshape(2, 128), jnp.zeros((2, 128), jnp.int32), trials])
        small.append(note if back == 0 else from_band(note, back))
    quarter_at = grp_at % 4
    residue = grp_at // 4

    def owned_by(owner):
        found = small[0] * 0
        for back in range(band_count):
            found = found + jnp.where((band_at - back) % band_count == owner, small[back], 0)
        return found

    quarter_subs = owned_by(quarter_at)[0:2].reshape(16, 16)
    subs = lax.dynamic_slice_in_dim(quarter_subs, residue, 1, axis=1).reshape(16) % 4
    all_delays = jnp.concatenate([owned_by(owner)[4:8] for owner in range(band_count)])

    chunks = spectra(voltages, band_at).reshape(64, 128, 128)
    turned = lax.all_to_all(chunks, "grp", split_axis=0, concat_axis=0, tiled=True)

    channels = quarter_at * 256 + 16 * jnp.arange(16, dtype=jnp.int32) + residue
    weights, east = beam_weights(channels)
    grid_at = steering[1] * 256 + steering[0]
    hot = (grid_at[:, None] == jnp.arange(1024, dtype=jnp.int32)[None, :]).astype(BF16)
    sums = beams(turned, east, subs, weights, hot).reshape(16, 64, 128)
    planes = [[4 * r + q for r in range(groups // 4)] for q in range(4)]
    pieces = lax.all_to_all(
        sums, "grp", split_axis=0, concat_axis=0, tiled=True, axis_index_groups=planes
    )
    columns = [
        [(4 * r + q) * band_count + band for q in range(4) for band in range(band_count)]
        for r in range(groups // 4)
    ]
    every = lax.all_to_all(
        gather_residues(pieces),
        ("grp", "band"),
        split_axis=0,
        concat_axis=0,
        tiled=True,
        axis_index_groups=columns,
    )
    return series(every, all_delays)


def solution(mesh):
    in_specs = (P("band", "grp", None), P(), P("band"), P(None, "band"))
    out_specs = P(None, "grp", "band")
    return jax.shard_map(local, mesh=mesh, in_specs=in_specs, out_specs=out_specs, check_vma=False)
```

```python
import math

import jax
import jax.numpy as jnp
import numpy as np
from jax import lax
from jax.experimental import pallas as pl
from jax.experimental.pallas import tpu as pltpu
from jax.sharding import PartitionSpec as P

A = 2048
FEEDS = 1024
C = 1024
SAMP = 2048
BEAMS = 1024
TRIALS = 512
F32 = jnp.float32
BF16 = jnp.bfloat16
MIB = 1 << 20
NT = (((1,), (1,)), ((), ()))
NN = (((1,), (0,)), ((), ()))


def window_taps():
    tap_pos = np.arange(4 * SAMP) + 0.5
    taper = 0.5 - 0.5 * np.cos(2.0 * np.pi / (4 * SAMP) * tap_pos)
    window = taper * np.sinc((tap_pos - 2 * SAMP) / SAMP)
    window = window * np.sqrt(SAMP / np.sum(window * window))
    return window.reshape(4, SAMP).astype(np.float32)


def lane_tables():
    k = np.arange(64)[:, None]
    lane = np.arange(128)[None, :]

    def rows(r, part):
        angle = 2.0 * np.pi / SAMP * (((16 * k + r) * lane) % SAMP)
        cos, sin = np.cos(angle) / np.sqrt(SAMP), np.sin(angle) / np.sqrt(SAMP)
        if part is not None:
            none = np.zeros_like(cos)
            pair = lambda x: np.concatenate([x, none] if part == 0 else [none, x], axis=1)
            return np.concatenate([pair(cos), pair(-sin)], axis=0)
        sign = -1.0 if r > 8 else 1.0
        top = np.concatenate([cos, -sin * sign], axis=1)
        return np.concatenate([top, np.concatenate([-sin, -cos * sign], axis=1)], axis=0)

    tables = [np.concatenate([rows(0, 0), rows(8, 1)], axis=0)]
    tables += [np.concatenate([rows(at, None), rows(16 - at, None)], axis=0) for at in range(1, 8)]
    return np.stack(tables).astype(jnp.bfloat16)


def real_dft16(x):
    h, c1, c3 = math.sqrt(0.5), math.cos(math.pi / 8), math.cos(3 * math.pi / 8)
    s = [x[j] + x[j + 8] for j in range(8)]
    d = [x[j] - x[j + 8] for j in range(8)]
    ss = [s[j] + s[j + 4] for j in range(4)]
    sd = [s[j] - s[j + 4] for j in range(4)]
    t0, t1 = ss[0] + ss[2], ss[1] + ss[3]
    out = [None] * 9
    out[0] = (t0 + t1, None)
    out[8] = (t0 - t1, None)
    out[4] = (ss[0] - ss[2], ss[1] - ss[3])
    dif, tot = h * (sd[1] - sd[3]), h * (sd[1] + sd[3])
    out[2] = (sd[0] + dif, sd[2] + tot)
    out[6] = (sd[0] - dif, tot - sd[2])
    p = [None] + [d[j] - d[8 - j] for j in (1, 2, 3)]
    q = [None] + [d[j] + d[8 - j] for j in (1, 2, 3)]
    hp, hq = h * p[2], h * q[2]
    ea, eb = d[0] + hp, d[0] - hp
    u, v = c1 * p[1] + c3 * p[3], c3 * p[1] - c1 * p[3]
    fa, fb = d[4] + hq, hq - d[4]
    y, z = c3 * q[1] + c1 * q[3], c1 * q[1] - c3 * q[3]
    out[1] = (ea + u, y + fa)
    out[7] = (ea - u, y - fa)
    out[3] = (eb + v, z + fb)
    out[5] = (eb - v, z - fb)
    return out


def frame_bins(part_ref, win_ref, row0, a0, frame, keep=None):
    lanes = []
    for jb in range(16):
        cols = slice(128 * jb, 128 * jb + 128)
        total = None
        for p in range(4):
            term = frame(p)[pl.ds(a0, 16), cols].astype(F32) * win_ref[p : p + 1, cols]
            if p == 3 and keep is not None:
                total = total * keep
            total = term if total is None else total + term
        lanes.append(total)
    rows = pl.ds(row0, 16)
    for at, (re, im) in enumerate(real_dft16(lanes)):
        if at % 8 == 0:
            part_ref[0, rows, 16 * at : 16 * at + 128] = re.astype(BF16)
        else:
            part_ref[at, rows, 0:128] = re.astype(BF16)
            part_ref[at, rows, 128:256] = im.astype(BF16)


def inner_kernel(v_ref, win_ref, part_ref):
    def body(step, carry):
        m = step // 2
        a0 = pl.multiple_of(16 * (step % 2), 16)
        frame_bins(part_ref, win_ref, pl.multiple_of(16 * step, 16), a0, lambda p: v_ref.at[m - 2 + p])
        return carry

    lax.fori_loop(4, 30, body, 0)


def spectra_kernel(
    band_ref, part_hbm, v_hbm, prev_ref, next_ref, win_ref, tab_hbm, out_hbm,
    part_ref, edge_ref, tab_ref, stage_ref, turn_ref, in_sem, out_sem
):
    inner = pl.ds(64, 416)
    first = pltpu.make_async_copy(v_hbm.at[0:3], edge_ref.at[0:3], in_sem.at[0])
    last = pltpu.make_async_copy(v_hbm.at[13:16], edge_ref.at[3:6], in_sem.at[1])
    parts = pltpu.make_async_copy(part_hbm.at[:, inner, :], part_ref.at[:, inner, :], in_sem.at[2])
    tables = pltpu.make_async_copy(tab_hbm, tab_ref, in_sem.at[3])
    for copy in (first, last, parts, tables):
        copy.start()
    keep = jnp.where(band_ref[0] == 3, 0.0, 1.0).astype(F32)
    first.wait()
    last.wait()

    def edge(half, carry):
        a0 = pl.multiple_of(16 * half, 16)
        for m in (0, 1):
            frame = lambda p, m=m: prev_ref.at[m + p] if m + p < 2 else edge_ref.at[m + p - 2]
            frame_bins(part_ref, win_ref, pl.multiple_of(32 * m + a0, 16), a0, frame)
        frame = lambda p: edge_ref.at[3 + p] if p < 3 else next_ref.at[0]
        frame_bins(part_ref, win_ref, pl.multiple_of(480 + a0, 16), a0, frame, keep)
        return carry

    lax.fori_loop(0, 2, edge, 0)
    parts.wait()
    tables.wait()
    sent = []
    for at in range(8):
        rows = lax.dot_general(tab_ref[at], part_ref[at], NT, preferred_element_type=F32)
        for which in range(2):
            slot = 2 * (at % 2) + which
            for reim in range(2):
                for mb in range(4):
                    r0 = 128 * which + 64 * reim
                    turn_ref[slot, pl.ds(reim * 4 + mb, 64, stride=8), :] = rows[
                        r0 : r0 + 64, 128 * mb : 128 * mb + 128
                    ]
        for which in range(2):
            slot = 2 * (at % 2) + which
            r = at if which == 0 else (8 if at == 0 else 16 - at)
            for q in range(4):
                stage_ref[r, q] = turn_ref[slot, 128 * q : 128 * q + 128, :].astype(BF16)
            copy = pltpu.make_async_copy(stage_ref.at[r], out_hbm.at[r], out_sem.at[r])
            copy.start()
            sent.append(copy)
    for copy in sent:
        copy.wait()


def spectra(voltages, band_at):
    band_count = lax.axis_size("band")
    ahead = lax.ppermute(voltages[14:16], "band", [(i, i + 1) for i in range(band_count - 1)])
    behind = lax.ppermute(voltages[0:1], "band", [(i, (i - 1) % band_count) for i in range(band_count)])
    window, tables = jnp.asarray(window_taps()), jnp.asarray(lane_tables())
    vmem, smem = pl.BlockSpec(memory_space=pltpu.VMEM), pl.BlockSpec(memory_space=pltpu.SMEM)
    anywhere = pl.BlockSpec(memory_space=pl.ANY)
    parts = pl.pallas_call(
        inner_kernel,
        name="inner_frames",
        out_shape=jax.ShapeDtypeStruct((8, 512, 256), BF16),
        in_specs=[vmem] * 2,
        out_specs=vmem,
        compiler_params=pltpu.CompilerParams(vmem_limit_bytes=58 * MIB),
        cost_estimate=pl.CostEstimate(flops=20_000_000, bytes_accessed=4_000_000, transcendentals=0),
    )(voltages, window)
    return pl.pallas_call(
        spectra_kernel,
        name="spectra",
        out_shape=jax.ShapeDtypeStruct((16, 4, 128, 128), BF16),
        in_specs=[smem, anywhere, anywhere, vmem, vmem, vmem, anywhere],
        out_specs=pl.BlockSpec(memory_space=pltpu.HBM),
        scratch_shapes=[
            pltpu.VMEM((8, 512, 256), BF16),
            pltpu.VMEM((6, 32, 2048), BF16),
            pltpu.VMEM((8, 256, 256), BF16),
            pltpu.VMEM((16, 4, 128, 128), BF16),
            pltpu.VMEM((4, 512, 128), F32),
            pltpu.SemaphoreType.DMA((4,)),
            pltpu.SemaphoreType.DMA((16,)),
        ],
        compiler_params=pltpu.CompilerParams(vmem_limit_bytes=52 * MIB),
        cost_estimate=pl.CostEstimate(
            flops=600_000_000, bytes_accessed=6_000_000, transcendentals=0
        ),
    )(band_at.reshape(1), parts, voltages, ahead, behind, window, tables)


def turn_blocks(tiles, axis, size):
    shape = tiles[0].shape
    at = lax.broadcasted_iota(jnp.int32, shape, axis) // size
    odd, high = at % 2 == 1, at // 2 == 1
    one = [None] * 4
    for a, b in ((0, 1), (2, 3)):
        one[a] = jnp.where(odd, pltpu.roll(tiles[b], size, axis), tiles[a])
        one[b] = jnp.where(odd, tiles[b], pltpu.roll(tiles[a], shape[axis] - size, axis))
    two = [None] * 4
    for a, b in ((0, 2), (1, 3)):
        two[a] = jnp.where(high, pltpu.roll(one[b], 2 * size, axis), one[a])
        two[b] = jnp.where(high, one[b], pltpu.roll(one[a], 2 * size, axis))
    return two


def place_channels(x_ref, left_ref):
    for pe in range(8):
        for h in range(2):
            src = pe * 8 + h * 4
            tiles = turn_blocks([x_ref[src + n] for n in range(4)], 1, 32)
            for m4 in range(4):
                rows = slice(16 * pe + 4 * m4, 16 * pe + 4 * m4 + 4)
                for ch in range(2):
                    for part in range(2):
                        cols = slice(256 * part + 128 * h, 256 * part + 128 * h + 128)
                        at = 8 * ch + 4 * part
                        left_ref[ch, rows, cols] = tiles[m4][at : at + 4]


def add_powers(channels, pair, east_ref, sub_ref, prod_ref, acc_ref):
    for ch in channels:
        i = 2 * pair + ch
        sub = sub_ref[i]
        cos = [[east_ref[i, s * 4 + k] for k in range(4)] for s in range(4)]
        sin = [[east_ref[i, 16 + s * 4 + k] for k in range(4)] for s in range(4)]
        for t in range(2):
            for h in range(2):
                total, corr_re, corr_im = None, [None] * 4, [None] * 4
                for p in range(2):
                    re, im = [], []
                    for e in range(4):
                        rows = slice(p * 64 + e * 16 + t * 8, p * 64 + e * 16 + t * 8 + 8)
                        re.append(prod_ref[ch, rows, 128 * h : 128 * h + 128])
                        im.append(prod_ref[ch, rows, 256 + 128 * h : 384 + 128 * h])
                    for e in range(4):
                        square = re[e] * re[e] + im[e] * im[e]
                        total = square if total is None else total + square
                    for k in range(1, 4):
                        for f in range(4 - k):
                            a = re[f + k] * re[f] + im[f + k] * im[f]
                            b = im[f + k] * re[f] - re[f + k] * im[f]
                            corr_re[k] = a if corr_re[k] is None else corr_re[k] + a
                            corr_im[k] = b if corr_im[k] is None else corr_im[k] + b
                for s in range(4):
                    if s == 0:
                        twice = corr_re[1] + corr_re[2] + corr_re[3]
                        power = total + (twice + twice)
                    else:
                        power = total
                        for k in range(1, 4):
                            power = power + (cos[s][k] * corr_re[k] - sin[s][k] * corr_im[k])
                    cols = slice(s * 256 + h * 128, s * 256 + h * 128 + 128)
                    acc_ref[sub, 8 * t : 8 * t + 8, cols] += power


def beam_kernel(
    east_ref, sub_ref, first_ref, odd_ref, next_ref, w_ref, hot_hbm, out_ref,
    left_ref, prod_ref, acc_ref, hot_ref, sem
):
    step = pl.program_id(0)
    fetch = pltpu.make_async_copy(hot_hbm, hot_ref, sem)
    block = [pl.when(sub_ref[0] >= 0) for at in range(4)]

    @pl.when(step == 0)
    def _():
        fetch.start()
        acc_ref[...] = jnp.zeros_like(acc_ref)
        prod_ref[...] = jnp.zeros_like(prod_ref)
        place_channels(first_ref, left_ref.at[0])

    def multiply(slot):
        for ch in range(2):
            prod_ref[slot, ch] = lax.dot_general(
                left_ref[slot, ch], w_ref[2 * slot + ch], NN, preferred_element_type=F32
            )

    def powers(channel, slot, pair):
        add_powers((channel,), pair, east_ref, sub_ref, prod_ref.at[slot], acc_ref)

    @block[0]
    def _():
        powers(0, 1, jnp.maximum(2 * step - 1, 0))
        multiply(0)

    @block[1]
    def _():
        powers(1, 1, jnp.maximum(2 * step - 1, 0))
        place_channels(odd_ref, left_ref.at[1])

    @block[2]
    def _():
        powers(0, 0, 2 * step)
        multiply(1)

    @block[3]
    def _():
        powers(1, 0, 2 * step)
        place_channels(next_ref, left_ref.at[0])

    @pl.when(step == pl.num_programs(0) - 1)
    def _():
        powers(0, 1, 2 * step + 1)
        powers(1, 1, 2 * step + 1)
        total = acc_ref[...].reshape(64, 1024)
        top = total.astype(BF16)
        rest = (total - top.astype(F32)).astype(BF16)
        parts = jnp.concatenate([top, rest], axis=0)
        fetch.wait()
        out_ref[...] = lax.dot_general(hot_ref[...], parts, NT, preferred_element_type=F32).astype(BF16)


def beams(turned, east, subs, weights, hot):
    smem = pl.BlockSpec(memory_space=pltpu.SMEM)
    return pl.pallas_call(
        beam_kernel,
        name="beams",
        grid=(4,),
        out_shape=jax.ShapeDtypeStruct((1024, 128), BF16),
        in_specs=[
            smem,
            smem,
            pl.BlockSpec((64, 16, 128), lambda i: (0, 0, 0)),
            pl.BlockSpec((64, 16, 128), lambda i: (0, 2 * i + 1, 0)),
            pl.BlockSpec((64, 16, 128), lambda i: (0, jnp.minimum(2 * i + 2, 7), 0)),
            pl.BlockSpec((4, 512, 512), lambda i: (i, 0, 0)),
            pl.BlockSpec(memory_space=pl.ANY),
        ],
        out_specs=pl.BlockSpec((1024, 128), lambda i: (0, 0)),
        scratch_shapes=[
            pltpu.VMEM((2, 2, 128, 512), BF16),
            pltpu.VMEM((2, 2, 128, 512), F32),
            pltpu.VMEM((4, 16, 1024), F32),
            pltpu.VMEM((1024, 1024), BF16),
            pltpu.SemaphoreType.DMA,
        ],
        compiler_params=pltpu.CompilerParams(vmem_limit_bytes=51 * MIB),
        cost_estimate=pl.CostEstimate(
            flops=2_000_000_000, bytes_accessed=13_000_000, transcendentals=0
        ),
    )(east, subs, turned, turned, turned, weights, hot)


def weight_kernel(step_ref, out_ref):
    scale = 2 * C * 256
    row = lax.broadcasted_iota(jnp.int32, (16, 256), 0)
    north = lax.broadcasted_iota(jnp.int32, (16, 256), 1)
    for ch in range(2):
        rate = step_ref[2 * pl.program_id(0) + ch]

        def turn(feeds):
            phases = (2.0 * math.pi / scale) * ((rate * (feeds * north)) % scale).astype(F32)
            return jnp.cos(phases), jnp.sin(phases)

        norm = 1.0 / math.sqrt(FEEDS)
        cos, sin = turn(row)
        cos, sin = cos * norm, sin * norm
        more_cos, more_sin = turn(16 + 0 * row)
        for tile in range(16):
            if tile:
                cos, sin = cos * more_cos - sin * more_sin, sin * more_cos + cos * more_sin
            top, low = slice(16 * tile, 16 * tile + 16), slice(256 + 16 * tile, 272 + 16 * tile)
            out_ref[ch, top, 0:256] = cos.astype(BF16)
            out_ref[ch, top, 256:512] = sin.astype(BF16)
            out_ref[ch, low, 0:256] = (-sin).astype(BF16)
            out_ref[ch, low, 256:512] = cos.astype(BF16)


def beam_weights(channels):
    scale = 2 * C
    steps = scale - channels
    weights = pl.pallas_call(
        weight_kernel,
        name="weights",
        grid=(8,),
        out_shape=jax.ShapeDtypeStruct((16, 512, 512), BF16),
        in_specs=[pl.BlockSpec(memory_space=pltpu.SMEM)],
        out_specs=pl.BlockSpec((2, 512, 512), lambda i: (i, 0, 0)),
        compiler_params=pltpu.CompilerParams(vmem_limit_bytes=56 * MIB),
        cost_estimate=pl.CostEstimate(flops=20_000_000, bytes_accessed=6_000_000, transcendentals=500_000),
    )(steps)
    four = jnp.arange(4, dtype=jnp.int32)
    turns = steps[:, None] * (four[:, None] * four[None, :]).reshape(1, 16) % (scale * 4)
    phases = (2.0 * math.pi / (scale * 4)) * turns.astype(F32)
    return weights, 2.0 * jnp.concatenate([jnp.cos(phases), jnp.sin(phases)], axis=1)


def gather_kernel(x_ref, out_ref):
    total = x_ref[0].astype(F32)
    for r in range(1, 16):
        total = total + x_ref[r].astype(F32)
    total = total + pltpu.roll(total, 64, 1)
    top = total.astype(BF16)
    rest = (total - top.astype(F32)).astype(BF16)
    lane = lax.broadcasted_iota(jnp.int32, (64, 128), 1)
    both = jnp.where(lane < 64, top, rest)
    for q in range(4):
        for band in range(4):
            out_ref[4 * q + band] = both[16 * q : 16 * q + 16, :]


def gather_residues(pieces):
    vmem = pl.BlockSpec(memory_space=pltpu.VMEM)
    return pl.pallas_call(
        gather_kernel,
        name="residues",
        out_shape=jax.ShapeDtypeStruct((16, 16, 128), BF16),
        in_specs=[vmem],
        out_specs=vmem,
        compiler_params=pltpu.CompilerParams(vmem_limit_bytes=4 * MIB),
    )(pieces)


def frame_tables():
    table = np.zeros((4, 2, 4, 4, 4, 4, 64), np.float32)
    for band in range(4):
        for m4 in range(4):
            for mb in range(4):
                row = np.full(64, -1.0 / 64.0)
                row[(16 * band + 1 + 4 * mb + m4) % 64] += 1.0
                for sub in range(4):
                    table[band, :, sub, m4, mb, sub, :] = row / math.sqrt(C)
    return table.reshape(4, 128, 256).astype(jnp.bfloat16)


def series_kernel(x_ref, tab_ref, delay_ref, out_ref, hot_ref, left_ref):
    series = None
    for band in range(4):
        rows = jnp.concatenate([x_ref[4 * q + band] for q in range(4)], axis=0)
        term = lax.dot_general(rows, tab_ref[band], NN, preferred_element_type=F32)
        series = term if series is None else series + term
    ahead = lax.broadcasted_iota(jnp.int32, (64, 128), 0)
    for s in range(16):
        hit = (ahead + delay_ref[s : s + 1, :]) % 64 == 0
        hot = jnp.where(hit, 1.0, 0.0).astype(BF16)
        for th in range(4):
            cols = slice(128 * th, 128 * th + 128)
            for tile in range(4):
                to = 64 * s + 16 * tile
                at = 16 * ((tile - th) % 4)
                hot_ref[to : to + 16, cols] = hot[at : at + 16, :]
    lane = lax.broadcasted_iota(jnp.int32, (16, 128), 1) % 64
    for at in range(8):
        rows, cols = slice(16 * (at // 2), 16 * (at // 2) + 16), slice(128 * (at % 2), 128 * (at % 2) + 128)
        block = series[rows, cols]
        for t in range(16):
            x = block
            if t:
                x = jnp.where(lane < 64 - t, pltpu.roll(x, 128 - t, 1), pltpu.roll(x, 64 - t, 1))
            top = x.astype(BF16)
            left_ref[0, 16 * t : 16 * t + 16, 128 * at : 128 * at + 128] = top
            left_ref[1, 16 * t : 16 * t + 16, 128 * at : 128 * at + 128] = (x - top.astype(F32)).astype(BF16)
    hot = hot_ref[...]
    out = lax.dot_general(left_ref[0], hot, NN, preferred_element_type=F32)
    out = out + lax.dot_general(left_ref[1], hot, NN, preferred_element_type=F32)
    for th in range(4):
        out_ref[16 * th : 16 * th + 16] = out[:, 128 * th : 128 * th + 128].reshape(16, 16, 128)


def series(sums, delays):
    vmem = pl.BlockSpec(memory_space=pltpu.VMEM)
    return pl.pallas_call(
        series_kernel,
        name="series",
        out_shape=jax.ShapeDtypeStruct((64, 16, 128), F32),
        in_specs=[vmem] * 3,
        out_specs=vmem,
        scratch_shapes=[pltpu.VMEM((1024, 512), BF16), pltpu.VMEM((2, 256, 1024), BF16)],
        compiler_params=pltpu.CompilerParams(vmem_limit_bytes=8 * MIB),
        cost_estimate=pl.CostEstimate(
            flops=600_000_000, bytes_accessed=1_000_000, transcendentals=0
        ),
    )(sums, jnp.asarray(frame_tables()), delays)


def from_band(block, back):
    count = lax.axis_size("band")
    return lax.ppermute(block, "band", [(i, (i + back) % count) for i in range(count)])


def local(voltages, steering, chan_sub, delays):
    groups, band_count = lax.axis_size("grp"), lax.axis_size("band")
    grp_at = lax.axis_index("grp")
    band_at = lax.axis_index("band")
    turned_delays = jnp.transpose(delays)
    small = []
    for back in range(band_count):
        trials = lax.dynamic_slice_in_dim(
            turned_delays, (band_at + back) % band_count * 128, 128, axis=1
        )
        note = jnp.concatenate([chan_sub.reshape(2, 128), jnp.zeros((2, 128), jnp.int32), trials])
        small.append(note if back == 0 else from_band(note, back))
    quarter_at = grp_at % 4
    residue = grp_at // 4

    def owned_by(owner):
        found = small[0] * 0
        for back in range(band_count):
            found = found + jnp.where((band_at - back) % band_count == owner, small[back], 0)
        return found

    quarter_subs = owned_by(quarter_at)[0:2].reshape(16, 16)
    subs = lax.dynamic_slice_in_dim(quarter_subs, residue, 1, axis=1).reshape(16) % 4
    all_delays = jnp.concatenate([owned_by(owner)[4:8] for owner in range(band_count)])

    chunks = spectra(voltages, band_at).reshape(64, 128, 128)
    turned = lax.all_to_all(chunks, "grp", split_axis=0, concat_axis=0, tiled=True)

    channels = quarter_at * 256 + 16 * jnp.arange(16, dtype=jnp.int32) + residue
    weights, east = beam_weights(channels)
    grid_at = steering[1] * 256 + steering[0]
    hot = (grid_at[:, None] == jnp.arange(1024, dtype=jnp.int32)[None, :]).astype(BF16)
    sums = beams(turned, east, subs, weights, hot).reshape(16, 64, 128)
    planes = [[4 * r + q for r in range(groups // 4)] for q in range(4)]
    pieces = lax.all_to_all(
        sums, "grp", split_axis=0, concat_axis=0, tiled=True, axis_index_groups=planes
    )
    columns = [
        [(4 * r + q) * band_count + band for q in range(4) for band in range(band_count)]
        for r in range(groups // 4)
    ]
    every = lax.all_to_all(
        gather_residues(pieces),
        ("grp", "band"),
        split_axis=0,
        concat_axis=0,
        tiled=True,
        axis_index_groups=columns,
    )
    return series(every, all_delays)


def solution(mesh):
    in_specs = (P("band", "grp", None), P(), P("band"), P(None, "band"))
    out_specs = P(None, "grp", "band")
    return jax.shard_map(local, mesh=mesh, in_specs=in_specs, out_specs=out_specs, check_vma=False)
```

```python
import math

import jax
import jax.numpy as jnp
import numpy as np
from jax import lax
from jax.experimental import pallas as pl
from jax.experimental.pallas import tpu as pltpu
from jax.sharding import PartitionSpec as P

A = 2048
FEEDS = 1024
C = 1024
SAMP = 2048
BEAMS = 1024
TRIALS = 512
F32 = jnp.float32
BF16 = jnp.bfloat16
MIB = 1 << 20
NT = (((1,), (1,)), ((), ()))
NN = (((1,), (0,)), ((), ()))


def window_taps():
    tap_pos = np.arange(4 * SAMP) + 0.5
    taper = 0.5 - 0.5 * np.cos(2.0 * np.pi / (4 * SAMP) * tap_pos)
    window = taper * np.sinc((tap_pos - 2 * SAMP) / SAMP)
    window = window * np.sqrt(SAMP / np.sum(window * window))
    return window.reshape(4, SAMP).astype(np.float32)


def lane_tables():
    k = np.arange(64)[:, None]
    lane = np.arange(128)[None, :]

    def rows(r, part):
        angle = 2.0 * np.pi / SAMP * (((16 * k + r) * lane) % SAMP)
        cos, sin = np.cos(angle) / np.sqrt(SAMP), np.sin(angle) / np.sqrt(SAMP)
        if part is not None:
            none = np.zeros_like(cos)
            pair = lambda x: np.concatenate([x, none] if part == 0 else [none, x], axis=1)
            return np.concatenate([pair(cos), pair(-sin)], axis=0)
        sign = -1.0 if r > 8 else 1.0
        top = np.concatenate([cos, -sin * sign], axis=1)
        return np.concatenate([top, np.concatenate([-sin, -cos * sign], axis=1)], axis=0)

    tables = [np.concatenate([rows(0, 0), rows(8, 1)], axis=0)]
    tables += [np.concatenate([rows(at, None), rows(16 - at, None)], axis=0) for at in range(1, 8)]
    return np.stack(tables).astype(jnp.bfloat16)


def real_dft16(x):
    h, c1, c3 = math.sqrt(0.5), math.cos(math.pi / 8), math.cos(3 * math.pi / 8)
    s = [x[j] + x[j + 8] for j in range(8)]
    d = [x[j] - x[j + 8] for j in range(8)]
    ss = [s[j] + s[j + 4] for j in range(4)]
    sd = [s[j] - s[j + 4] for j in range(4)]
    t0, t1 = ss[0] + ss[2], ss[1] + ss[3]
    out = [None] * 9
    out[0] = (t0 + t1, None)
    out[8] = (t0 - t1, None)
    out[4] = (ss[0] - ss[2], ss[1] - ss[3])
    dif, tot = h * (sd[1] - sd[3]), h * (sd[1] + sd[3])
    out[2] = (sd[0] + dif, sd[2] + tot)
    out[6] = (sd[0] - dif, tot - sd[2])
    p = [None] + [d[j] - d[8 - j] for j in (1, 2, 3)]
    q = [None] + [d[j] + d[8 - j] for j in (1, 2, 3)]
    hp, hq = h * p[2], h * q[2]
    ea, eb = d[0] + hp, d[0] - hp
    u, v = c1 * p[1] + c3 * p[3], c3 * p[1] - c1 * p[3]
    fa, fb = d[4] + hq, hq - d[4]
    y, z = c3 * q[1] + c1 * q[3], c1 * q[1] - c3 * q[3]
    out[1] = (ea + u, y + fa)
    out[7] = (ea - u, y - fa)
    out[3] = (eb + v, z + fb)
    out[5] = (eb - v, z - fb)
    return out


def frame_bins(part_ref, win_ref, row0, a0, frame, keep=None):
    lanes = []
    for jb in range(16):
        cols = slice(128 * jb, 128 * jb + 128)
        total = None
        for p in range(4):
            term = frame(p)[pl.ds(a0, 16), cols].astype(F32) * win_ref[p : p + 1, cols]
            if p == 3 and keep is not None:
                total = total * keep
            total = term if total is None else total + term
        lanes.append(total)
    rows = pl.ds(row0, 16)
    for at, (re, im) in enumerate(real_dft16(lanes)):
        if at % 8 == 0:
            part_ref[0, rows, 16 * at : 16 * at + 128] = re.astype(BF16)
        else:
            part_ref[at, rows, 0:128] = re.astype(BF16)
            part_ref[at, rows, 128:256] = im.astype(BF16)


def inner_kernel(v_ref, win_ref, part_ref):
    def body(step, carry):
        m = step // 2
        a0 = pl.multiple_of(16 * (step % 2), 16)
        frame_bins(part_ref, win_ref, pl.multiple_of(16 * step, 16), a0, lambda p: v_ref.at[m - 2 + p])
        return carry

    lax.fori_loop(4, 30, body, 0)


def spectra_kernel(
    band_ref, part_hbm, v_hbm, prev_ref, next_ref, win_ref, tab_hbm, out_hbm,
    part_ref, edge_ref, tab_ref, stage_ref, turn_ref, in_sem, out_sem
):
    inner = pl.ds(64, 416)
    first = pltpu.make_async_copy(v_hbm.at[0:3], edge_ref.at[0:3], in_sem.at[0])
    last = pltpu.make_async_copy(v_hbm.at[13:16], edge_ref.at[3:6], in_sem.at[1])
    parts = pltpu.make_async_copy(part_hbm.at[:, inner, :], part_ref.at[:, inner, :], in_sem.at[2])
    tables = pltpu.make_async_copy(tab_hbm, tab_ref, in_sem.at[3])
    for copy in (first, last, parts, tables):
        copy.start()
    keep = jnp.where(band_ref[0] == 3, 0.0, 1.0).astype(F32)
    first.wait()
    last.wait()

    def edge(half, carry):
        a0 = pl.multiple_of(16 * half, 16)
        for m in (0, 1):
            frame = lambda p, m=m: prev_ref.at[m + p] if m + p < 2 else edge_ref.at[m + p - 2]
            frame_bins(part_ref, win_ref, pl.multiple_of(32 * m + a0, 16), a0, frame)
        frame = lambda p: edge_ref.at[3 + p] if p < 3 else next_ref.at[0]
        frame_bins(part_ref, win_ref, pl.multiple_of(480 + a0, 16), a0, frame, keep)
        return carry

    lax.fori_loop(0, 2, edge, 0)
    parts.wait()
    tables.wait()
    sent = []
    for at in range(8):
        rows = lax.dot_general(tab_ref[at], part_ref[at], NT, preferred_element_type=F32)
        for which in range(2):
            slot = 2 * (at % 2) + which
            for reim in range(2):
                for mb in range(4):
                    r0 = 128 * which + 64 * reim
                    turn_ref[slot, pl.ds(reim * 4 + mb, 64, stride=8), :] = rows[
                        r0 : r0 + 64, 128 * mb : 128 * mb + 128
                    ]
        for which in range(2):
            slot = 2 * (at % 2) + which
            r = at if which == 0 else (8 if at == 0 else 16 - at)
            for q in range(4):
                stage_ref[r, q] = turn_ref[slot, 128 * q : 128 * q + 128, :].astype(BF16)
            copy = pltpu.make_async_copy(stage_ref.at[r], out_hbm.at[r], out_sem.at[r])
            copy.start()
            sent.append(copy)
    for copy in sent:
        copy.wait()


def spectra(voltages, band_at):
    band_count = lax.axis_size("band")
    ahead = lax.ppermute(voltages[14:16], "band", [(i, i + 1) for i in range(band_count - 1)])
    behind = lax.ppermute(voltages[0:1], "band", [(i, (i - 1) % band_count) for i in range(band_count)])
    window, tables = jnp.asarray(window_taps()), jnp.asarray(lane_tables())
    vmem, smem = pl.BlockSpec(memory_space=pltpu.VMEM), pl.BlockSpec(memory_space=pltpu.SMEM)
    anywhere = pl.BlockSpec(memory_space=pl.ANY)
    parts = pl.pallas_call(
        inner_kernel,
        name="inner_frames",
        out_shape=jax.ShapeDtypeStruct((8, 512, 256), BF16),
        in_specs=[vmem] * 2,
        out_specs=vmem,
        compiler_params=pltpu.CompilerParams(vmem_limit_bytes=58 * MIB),
        cost_estimate=pl.CostEstimate(flops=20_000_000, bytes_accessed=4_000_000, transcendentals=0),
    )(voltages, window)
    return pl.pallas_call(
        spectra_kernel,
        name="spectra",
        out_shape=jax.ShapeDtypeStruct((16, 4, 128, 128), BF16),
        in_specs=[smem, anywhere, anywhere, vmem, vmem, vmem, anywhere],
        out_specs=pl.BlockSpec(memory_space=pltpu.HBM),
        scratch_shapes=[
            pltpu.VMEM((8, 512, 256), BF16),
            pltpu.VMEM((6, 32, 2048), BF16),
            pltpu.VMEM((8, 256, 256), BF16),
            pltpu.VMEM((16, 4, 128, 128), BF16),
            pltpu.VMEM((4, 512, 128), F32),
            pltpu.SemaphoreType.DMA((4,)),
            pltpu.SemaphoreType.DMA((16,)),
        ],
        compiler_params=pltpu.CompilerParams(vmem_limit_bytes=52 * MIB),
        cost_estimate=pl.CostEstimate(
            flops=600_000_000, bytes_accessed=6_000_000, transcendentals=0
        ),
    )(band_at.reshape(1), parts, voltages, ahead, behind, window, tables)


def turn_blocks(tiles, axis, size):
    shape = tiles[0].shape
    at = lax.broadcasted_iota(jnp.int32, shape, axis) // size
    odd, high = at % 2 == 1, at // 2 == 1
    one = [None] * 4
    for a, b in ((0, 1), (2, 3)):
        one[a] = jnp.where(odd, pltpu.roll(tiles[b], size, axis), tiles[a])
        one[b] = jnp.where(odd, tiles[b], pltpu.roll(tiles[a], shape[axis] - size, axis))
    two = [None] * 4
    for a, b in ((0, 2), (1, 3)):
        two[a] = jnp.where(high, pltpu.roll(one[b], 2 * size, axis), one[a])
        two[b] = jnp.where(high, one[b], pltpu.roll(one[a], 2 * size, axis))
    return two


def place_channels(x_ref, left_ref):
    for pe in range(8):
        for h in range(2):
            src = pe * 8 + h * 4
            tiles = turn_blocks([x_ref[src + n] for n in range(4)], 1, 32)
            for m4 in range(4):
                rows = slice(16 * pe + 4 * m4, 16 * pe + 4 * m4 + 4)
                for ch in range(2):
                    for part in range(2):
                        cols = slice(256 * part + 128 * h, 256 * part + 128 * h + 128)
                        at = 8 * ch + 4 * part
                        left_ref[ch, rows, cols] = tiles[m4][at : at + 4]


def add_powers(channels, pair, east_ref, chan_ref, residue_ref, prod_ref, acc_ref):
    for ch in channels:
        i = 2 * pair + ch
        sub = chan_ref[16 * i + residue_ref[0]] % 4
        cos = [[east_ref[i, s * 4 + k] for k in range(4)] for s in range(4)]
        sin = [[east_ref[i, 16 + s * 4 + k] for k in range(4)] for s in range(4)]
        for t in range(2):
            for h in range(2):
                total, corr_re, corr_im = None, [None] * 4, [None] * 4
                for p in range(2):
                    re, im = [], []
                    for e in range(4):
                        rows = slice(p * 64 + e * 16 + t * 8, p * 64 + e * 16 + t * 8 + 8)
                        re.append(prod_ref[ch, rows, 128 * h : 128 * h + 128])
                        im.append(prod_ref[ch, rows, 256 + 128 * h : 384 + 128 * h])
                    for e in range(4):
                        square = re[e] * re[e] + im[e] * im[e]
                        total = square if total is None else total + square
                    for k in range(1, 4):
                        for f in range(4 - k):
                            a = re[f + k] * re[f] + im[f + k] * im[f]
                            b = im[f + k] * re[f] - re[f + k] * im[f]
                            corr_re[k] = a if corr_re[k] is None else corr_re[k] + a
                            corr_im[k] = b if corr_im[k] is None else corr_im[k] + b
                for s in range(4):
                    if s == 0:
                        twice = corr_re[1] + corr_re[2] + corr_re[3]
                        power = total + (twice + twice)
                    else:
                        power = total
                        for k in range(1, 4):
                            power = power + (cos[s][k] * corr_re[k] - sin[s][k] * corr_im[k])
                    cols = slice(s * 256 + h * 128, s * 256 + h * 128 + 128)
                    acc_ref[sub, 8 * t : 8 * t + 8, cols] += power


def beam_kernel(
    east_ref, chan_ref, residue_ref, first_ref, odd_ref, next_ref, w_hbm, hot_hbm, out_ref,
    left_ref, prod_ref, acc_ref, w_ref, hot_ref, w_sem, sem
):
    step = pl.program_id(0)
    fetch = pltpu.make_async_copy(hot_hbm, hot_ref, sem)

    def weights(at):
        four = pl.ds(4 * at, 4)
        return pltpu.make_async_copy(w_hbm.at[four], w_ref.at[four], w_sem.at[at])

    block = [pl.when(chan_ref[0] >= 0) for at in range(4)]

    @pl.when(step == 0)
    def _():
        for at in range(4):
            weights(at).start()
        fetch.start()
        acc_ref[...] = jnp.zeros_like(acc_ref)
        prod_ref[...] = jnp.zeros_like(prod_ref)
        place_channels(first_ref, left_ref.at[0])

    weights(step).wait()

    def multiply(slot):
        for ch in range(2):
            prod_ref[slot, ch] = lax.dot_general(
                left_ref[slot, ch], w_ref[4 * step + 2 * slot + ch], NN, preferred_element_type=F32
            )

    def powers(channel, slot, pair):
        add_powers((channel,), pair, east_ref, chan_ref, residue_ref, prod_ref.at[slot], acc_ref)

    @block[0]
    def _():
        powers(0, 1, jnp.maximum(2 * step - 1, 0))
        multiply(0)

    @block[1]
    def _():
        powers(1, 1, jnp.maximum(2 * step - 1, 0))
        place_channels(odd_ref, left_ref.at[1])

    @block[2]
    def _():
        powers(0, 0, 2 * step)
        multiply(1)

    @block[3]
    def _():
        powers(1, 0, 2 * step)
        place_channels(next_ref, left_ref.at[0])

    @pl.when(step == pl.num_programs(0) - 1)
    def _():
        powers(0, 1, 2 * step + 1)
        powers(1, 1, 2 * step + 1)
        total = acc_ref[...].reshape(64, 1024)
        top = total.astype(BF16)
        rest = (total - top.astype(F32)).astype(BF16)
        parts = jnp.concatenate([top, rest], axis=0)
        fetch.wait()
        out_ref[...] = lax.dot_general(hot_ref[...], parts, NT, preferred_element_type=F32).astype(BF16)


def beams(turned, east, chan_sub, residue, weights, hot):
    smem = pl.BlockSpec(memory_space=pltpu.SMEM)
    return pl.pallas_call(
        beam_kernel,
        name="beams",
        grid=(4,),
        out_shape=jax.ShapeDtypeStruct((1024, 128), BF16),
        in_specs=[
            smem,
            smem,
            smem,
            pl.BlockSpec((64, 16, 128), lambda i: (0, 0, 0)),
            pl.BlockSpec((64, 16, 128), lambda i: (0, 2 * i + 1, 0)),
            pl.BlockSpec((64, 16, 128), lambda i: (0, jnp.minimum(2 * i + 2, 7), 0)),
            pl.BlockSpec(memory_space=pl.ANY),
            pl.BlockSpec(memory_space=pl.ANY),
        ],
        out_specs=pl.BlockSpec((1024, 128), lambda i: (0, 0)),
        scratch_shapes=[
            pltpu.VMEM((2, 2, 128, 512), BF16),
            pltpu.VMEM((2, 2, 128, 512), F32),
            pltpu.VMEM((4, 16, 1024), F32),
            pltpu.VMEM((16, 512, 512), BF16),
            pltpu.VMEM((1024, 1024), BF16),
            pltpu.SemaphoreType.DMA((4,)),
            pltpu.SemaphoreType.DMA,
        ],
        compiler_params=pltpu.CompilerParams(vmem_limit_bytes=51 * MIB),
        cost_estimate=pl.CostEstimate(
            flops=2_000_000_000, bytes_accessed=13_000_000, transcendentals=0
        ),
    )(east, chan_sub, residue.reshape(1), turned, turned, turned, weights, hot)


def weight_kernel(step_ref, out_ref):
    scale = 2 * C * 256
    row = lax.broadcasted_iota(jnp.int32, (16, 256), 0)
    north = lax.broadcasted_iota(jnp.int32, (16, 256), 1)
    for ch in range(2):
        rate = step_ref[2 * pl.program_id(0) + ch]

        def turn(feeds):
            phases = (2.0 * math.pi / scale) * ((rate * (feeds * north)) % scale).astype(F32)
            return jnp.cos(phases), jnp.sin(phases)

        norm = 1.0 / math.sqrt(FEEDS)
        cos, sin = turn(row)
        cos, sin = cos * norm, sin * norm
        more_cos, more_sin = turn(16 + 0 * row)
        for tile in range(16):
            if tile:
                cos, sin = cos * more_cos - sin * more_sin, sin * more_cos + cos * more_sin
            top, low = slice(16 * tile, 16 * tile + 16), slice(256 + 16 * tile, 272 + 16 * tile)
            out_ref[ch, top, 0:256] = cos.astype(BF16)
            out_ref[ch, top, 256:512] = sin.astype(BF16)
            out_ref[ch, low, 0:256] = (-sin).astype(BF16)
            out_ref[ch, low, 256:512] = cos.astype(BF16)


def beam_weights(channels):
    scale = 2 * C
    steps = scale - channels
    weights = pl.pallas_call(
        weight_kernel,
        name="weights",
        grid=(8,),
        out_shape=jax.ShapeDtypeStruct((16, 512, 512), BF16),
        in_specs=[pl.BlockSpec(memory_space=pltpu.SMEM)],
        out_specs=pl.BlockSpec((2, 512, 512), lambda i: (i, 0, 0)),
        compiler_params=pltpu.CompilerParams(vmem_limit_bytes=56 * MIB),
        cost_estimate=pl.CostEstimate(flops=20_000_000, bytes_accessed=6_000_000, transcendentals=500_000),
    )(steps)
    four = jnp.arange(4, dtype=jnp.int32)
    turns = steps[:, None] * (four[:, None] * four[None, :]).reshape(1, 16) % (scale * 4)
    phases = (2.0 * math.pi / (scale * 4)) * turns.astype(F32)
    return weights, 2.0 * jnp.concatenate([jnp.cos(phases), jnp.sin(phases)], axis=1)


def gather_kernel(x_ref, delay_ref, out_ref):
    total = x_ref[0].astype(F32)
    for r in range(1, 16):
        total = total + x_ref[r].astype(F32)
    total = total + pltpu.roll(total, 64, 1)
    top = total.astype(BF16)
    rest = (total - top.astype(F32)).astype(BF16)
    lane = lax.broadcasted_iota(jnp.int32, (64, 128), 1)
    both = jnp.where(lane < 64, top, rest)
    for q in range(4):
        for band in range(4):
            out_ref[4 * q + band, 0:16] = both[16 * q : 16 * q + 16, :]
            out_ref[4 * q + band, 16:24] = delay_ref[band]


def gather_residues(pieces, delays):
    vmem = pl.BlockSpec(memory_space=pltpu.VMEM)
    return pl.pallas_call(
        gather_kernel,
        name="residues",
        out_shape=jax.ShapeDtypeStruct((16, 24, 128), BF16),
        in_specs=[vmem] * 2,
        out_specs=vmem,
        compiler_params=pltpu.CompilerParams(vmem_limit_bytes=4 * MIB),
    )(pieces, delays)


def frame_tables():
    table = np.zeros((4, 2, 4, 4, 4, 4, 64), np.float32)
    for band in range(4):
        for m4 in range(4):
            for mb in range(4):
                row = np.full(64, -1.0 / 64.0)
                row[(16 * band + 1 + 4 * mb + m4) % 64] += 1.0
                for sub in range(4):
                    table[band, :, sub, m4, mb, sub, :] = row / math.sqrt(C)
    return table.reshape(4, 128, 256).astype(jnp.bfloat16)


def series_kernel(x_ref, tab_ref, out_ref, hot_ref, left_ref):
    series = None
    for band in range(4):
        rows = jnp.concatenate([x_ref[4 * q + band, 0:16] for q in range(4)], axis=0)
        term = lax.dot_general(rows, tab_ref[band], NN, preferred_element_type=F32)
        series = term if series is None else series + term
    ahead = lax.broadcasted_iota(jnp.int32, (64, 128), 0)
    delays = [x_ref[band, 16:24].astype(F32).astype(jnp.int32) for band in range(4)]
    for s in range(16):
        hit = (ahead + delays[s // 4][s % 4 : s % 4 + 1, :]) % 64 == 0
        hot = jnp.where(hit, 1.0, 0.0).astype(BF16)
        for th in range(4):
            cols = slice(128 * th, 128 * th + 128)
            for tile in range(4):
                to = 64 * s + 16 * tile
                at = 16 * ((tile - th) % 4)
                hot_ref[to : to + 16, cols] = hot[at : at + 16, :]
    lane = lax.broadcasted_iota(jnp.int32, (16, 128), 1) % 64
    for at in range(8):
        rows, cols = slice(16 * (at // 2), 16 * (at // 2) + 16), slice(128 * (at % 2), 128 * (at % 2) + 128)
        block = series[rows, cols]
        for t in range(16):
            x = block
            if t:
                x = jnp.where(lane < 64 - t, pltpu.roll(x, 128 - t, 1), pltpu.roll(x, 64 - t, 1))
            top = x.astype(BF16)
            left_ref[0, 16 * t : 16 * t + 16, 128 * at : 128 * at + 128] = top
            left_ref[1, 16 * t : 16 * t + 16, 128 * at : 128 * at + 128] = (x - top.astype(F32)).astype(BF16)
    hot = hot_ref[...]
    out = lax.dot_general(left_ref[0], hot, NN, preferred_element_type=F32)
    out = out + lax.dot_general(left_ref[1], hot, NN, preferred_element_type=F32)
    for th in range(4):
        out_ref[16 * th : 16 * th + 16] = out[:, 128 * th : 128 * th + 128].reshape(16, 16, 128)


def series(sums):
    vmem = pl.BlockSpec(memory_space=pltpu.VMEM)
    return pl.pallas_call(
        series_kernel,
        name="series",
        out_shape=jax.ShapeDtypeStruct((64, 16, 128), F32),
        in_specs=[vmem] * 2,
        out_specs=vmem,
        scratch_shapes=[pltpu.VMEM((1024, 512), BF16), pltpu.VMEM((2, 256, 1024), BF16)],
        compiler_params=pltpu.CompilerParams(vmem_limit_bytes=8 * MIB),
        cost_estimate=pl.CostEstimate(
            flops=600_000_000, bytes_accessed=1_000_000, transcendentals=0
        ),
    )(sums, jnp.asarray(frame_tables()))


def local(voltages, steering, chan_sub, delays):
    groups, band_count = lax.axis_size("grp"), lax.axis_size("band")
    grp_at = lax.axis_index("grp")
    band_at = lax.axis_index("band")
    quarter_at = grp_at % 4
    residue = grp_at // 4

    chunks = spectra(voltages, band_at).reshape(64, 128, 128)
    turned = lax.all_to_all(chunks, "grp", split_axis=0, concat_axis=0, tiled=True)

    place = lambda r, q, b: (4 * r + q) * band_count + b
    swap = [
        (place(r, q, b), place(r, b, q))
        for r in range(groups // 4)
        for q in range(4)
        for b in range(band_count)
    ]
    quarter_subs = lax.ppermute(chan_sub, ("grp", "band"), swap)
    channels = quarter_at * 256 + 16 * jnp.arange(16, dtype=jnp.int32) + residue
    weights, east = beam_weights(channels)
    grid_at = steering[1] * 256 + steering[0]
    hot = (grid_at[:, None] == jnp.arange(1024, dtype=jnp.int32)[None, :]).astype(BF16)
    notes = jnp.transpose(delays.reshape(band_count, 128, 4), (0, 2, 1)).astype(BF16)
    notes = jnp.pad(notes, ((0, 0), (0, 4), (0, 0)))
    sums = beams(turned, east, quarter_subs, residue, weights, hot).reshape(16, 64, 128)
    planes = [[4 * r + q for r in range(groups // 4)] for q in range(4)]
    pieces = lax.all_to_all(
        sums, "grp", split_axis=0, concat_axis=0, tiled=True, axis_index_groups=planes
    )
    columns = [
        [place(r, q, b) for q in range(4) for b in range(band_count)] for r in range(groups // 4)
    ]
    every = lax.all_to_all(
        gather_residues(pieces, notes),
        ("grp", "band"),
        split_axis=0,
        concat_axis=0,
        tiled=True,
        axis_index_groups=columns,
    )
    return series(every)


def solution(mesh):
    in_specs = (P("band", "grp", None), P(), P("band"), P(None, "band"))
    out_specs = P(None, "grp", "band")
    return jax.shard_map(local, mesh=mesh, in_specs=in_specs, out_specs=out_specs, check_vma=False)
```

```python
import math

import jax
import jax.numpy as jnp
import numpy as np
from jax import lax
from jax.experimental import pallas as pl
from jax.experimental.pallas import tpu as pltpu
from jax.sharding import PartitionSpec as P


FEEDS = 1024
C = 1024
SAMP = 2048
F32 = jnp.float32
BF16 = jnp.bfloat16
MIB = 1 << 20
NT = (((1,), (1,)), ((), ()))
NN = (((1,), (0,)), ((), ()))


def window_taps():
    tap_pos = np.arange(4 * SAMP) + 0.5
    taper = 0.5 - 0.5 * np.cos(2.0 * np.pi / (4 * SAMP) * tap_pos)
    window = taper * np.sinc((tap_pos - 2 * SAMP) / SAMP)
    window = window * np.sqrt(SAMP / np.sum(window * window))
    return window.reshape(4, SAMP).astype(np.float32)


def lane_tables():
    k = np.arange(64)[:, None]
    lane = np.arange(128)[None, :]

    def rows(r, part):
        angle = 2.0 * np.pi / SAMP * (((16 * k + r) * lane) % SAMP)
        cos, sin = np.cos(angle) / np.sqrt(SAMP), np.sin(angle) / np.sqrt(SAMP)
        if part is not None:
            none = np.zeros_like(cos)
            pair = lambda x: np.concatenate([x, none] if part == 0 else [none, x], axis=1)
            return np.concatenate([pair(cos), pair(-sin)], axis=0)
        sign = -1.0 if r > 8 else 1.0
        top = np.concatenate([cos, -sin * sign], axis=1)
        return np.concatenate([top, np.concatenate([-sin, -cos * sign], axis=1)], axis=0)

    tables = [np.concatenate([rows(0, 0), rows(8, 1)], axis=0)]
    tables += [np.concatenate([rows(at, None), rows(16 - at, None)], axis=0) for at in range(1, 8)]
    return np.stack(tables).astype(jnp.bfloat16)


def real_dft16(x):
    h, c1, c3 = math.sqrt(0.5), math.cos(math.pi / 8), math.cos(3 * math.pi / 8)
    s = [x[j] + x[j + 8] for j in range(8)]
    d = [x[j] - x[j + 8] for j in range(8)]
    ss = [s[j] + s[j + 4] for j in range(4)]
    sd = [s[j] - s[j + 4] for j in range(4)]
    t0, t1 = ss[0] + ss[2], ss[1] + ss[3]
    out = [None] * 9
    out[0] = (t0 + t1, None)
    out[8] = (t0 - t1, None)
    out[4] = (ss[0] - ss[2], ss[1] - ss[3])
    dif, tot = h * (sd[1] - sd[3]), h * (sd[1] + sd[3])
    out[2] = (sd[0] + dif, sd[2] + tot)
    out[6] = (sd[0] - dif, tot - sd[2])
    p = [None] + [d[j] - d[8 - j] for j in (1, 2, 3)]
    q = [None] + [d[j] + d[8 - j] for j in (1, 2, 3)]
    hp, hq = h * p[2], h * q[2]
    ea, eb = d[0] + hp, d[0] - hp
    u, v = c1 * p[1] + c3 * p[3], c3 * p[1] - c1 * p[3]
    fa, fb = d[4] + hq, hq - d[4]
    y, z = c3 * q[1] + c1 * q[3], c1 * q[1] - c3 * q[3]
    out[1] = (ea + u, y + fa)
    out[7] = (ea - u, y - fa)
    out[3] = (eb + v, z + fb)
    out[5] = (eb - v, z - fb)
    return out


def frame_bins(part_ref, win_ref, row0, a0, frame, keep=None):
    lanes = []
    for jb in range(16):
        cols = slice(128 * jb, 128 * jb + 128)
        total = None
        for p in range(4):
            term = frame(p)[pl.ds(a0, 16), cols].astype(F32) * win_ref[p : p + 1, cols]
            if p == 3 and keep is not None:
                total = total * keep
            total = term if total is None else total + term
        lanes.append(total)
    rows = pl.ds(row0, 16)
    for at, (re, im) in enumerate(real_dft16(lanes)):
        if at % 8 == 0:
            part_ref[0, rows, 16 * at : 16 * at + 128] = re.astype(BF16)
        else:
            part_ref[at, rows, 0:128] = re.astype(BF16)
            part_ref[at, rows, 128:256] = im.astype(BF16)


def inner_kernel(v_ref, win_ref, part_ref):
    def body(step, carry):
        m = step // 2
        a0 = pl.multiple_of(16 * (step % 2), 16)
        frame_bins(part_ref, win_ref, pl.multiple_of(16 * step, 16), a0, lambda p: v_ref.at[m - 2 + p])
        return carry

    lax.fori_loop(4, 30, body, 0)


def spectra_kernel(
    band_ref, part_hbm, v_hbm, prev_ref, next_ref, win_ref, tab_hbm, out_hbm,
    part_ref, edge_ref, tab_ref, stage_ref, turn_ref, in_sem, out_sem
):
    inner = pl.ds(64, 416)
    first = pltpu.make_async_copy(v_hbm.at[0:3], edge_ref.at[0:3], in_sem.at[0])
    last = pltpu.make_async_copy(v_hbm.at[13:16], edge_ref.at[3:6], in_sem.at[1])
    parts = pltpu.make_async_copy(part_hbm.at[:, inner, :], part_ref.at[:, inner, :], in_sem.at[2])
    tables = pltpu.make_async_copy(tab_hbm, tab_ref, in_sem.at[3])
    for copy in (first, last, parts, tables):
        copy.start()
    keep = jnp.where(band_ref[0] == 3, 0.0, 1.0).astype(F32)
    first.wait()
    last.wait()

    def edge(half, carry):
        a0 = pl.multiple_of(16 * half, 16)
        for m in (0, 1):
            frame = lambda p, m=m: prev_ref.at[m + p] if m + p < 2 else edge_ref.at[m + p - 2]
            frame_bins(part_ref, win_ref, pl.multiple_of(32 * m + a0, 16), a0, frame)
        frame = lambda p: edge_ref.at[3 + p] if p < 3 else next_ref.at[0]
        frame_bins(part_ref, win_ref, pl.multiple_of(480 + a0, 16), a0, frame, keep)
        return carry

    lax.fori_loop(0, 2, edge, 0)
    parts.wait()
    tables.wait()
    sent = []
    for at in range(8):
        rows = lax.dot_general(tab_ref[at], part_ref[at], NT, preferred_element_type=F32)
        for which in range(2):
            slot = 2 * (at % 2) + which
            for reim in range(2):
                for mb in range(4):
                    r0 = 128 * which + 64 * reim
                    turn_ref[slot, pl.ds(reim * 4 + mb, 64, stride=8), :] = rows[
                        r0 : r0 + 64, 128 * mb : 128 * mb + 128
                    ]
        for which in range(2):
            slot = 2 * (at % 2) + which
            r = at if which == 0 else (8 if at == 0 else 16 - at)
            for q in range(4):
                stage_ref[r, q] = turn_ref[slot, 128 * q : 128 * q + 128, :].astype(BF16)
            copy = pltpu.make_async_copy(stage_ref.at[r], out_hbm.at[r], out_sem.at[r])
            copy.start()
            sent.append(copy)
    for copy in sent:
        copy.wait()


def spectra(voltages, band_at):
    band_count = lax.axis_size("band")
    ahead = lax.ppermute(voltages[14:16], "band", [(i, i + 1) for i in range(band_count - 1)])
    behind = lax.ppermute(voltages[0:1], "band", [(i, (i - 1) % band_count) for i in range(band_count)])
    window, tables = jnp.asarray(window_taps()), jnp.asarray(lane_tables())
    vmem, smem = pl.BlockSpec(memory_space=pltpu.VMEM), pl.BlockSpec(memory_space=pltpu.SMEM)
    anywhere = pl.BlockSpec(memory_space=pl.ANY)
    parts = pl.pallas_call(
        inner_kernel,
        name="inner_frames",
        out_shape=jax.ShapeDtypeStruct((8, 512, 256), BF16),
        in_specs=[vmem] * 2,
        out_specs=vmem,
        compiler_params=pltpu.CompilerParams(vmem_limit_bytes=58 * MIB),
        cost_estimate=pl.CostEstimate(flops=20_000_000, bytes_accessed=4_000_000, transcendentals=0),
    )(voltages, window)
    return pl.pallas_call(
        spectra_kernel,
        name="spectra",
        out_shape=jax.ShapeDtypeStruct((16, 4, 128, 128), BF16),
        in_specs=[smem, anywhere, anywhere, vmem, vmem, vmem, anywhere],
        out_specs=pl.BlockSpec(memory_space=pltpu.HBM),
        scratch_shapes=[
            pltpu.VMEM((8, 512, 256), BF16),
            pltpu.VMEM((6, 32, 2048), BF16),
            pltpu.VMEM((8, 256, 256), BF16),
            pltpu.VMEM((16, 4, 128, 128), BF16),
            pltpu.VMEM((4, 512, 128), F32),
            pltpu.SemaphoreType.DMA((4,)),
            pltpu.SemaphoreType.DMA((16,)),
        ],
        compiler_params=pltpu.CompilerParams(vmem_limit_bytes=52 * MIB),
        cost_estimate=pl.CostEstimate(
            flops=600_000_000, bytes_accessed=6_000_000, transcendentals=0
        ),
    )(band_at.reshape(1), parts, voltages, ahead, behind, window, tables)


def turn_blocks(tiles, axis, size):
    shape = tiles[0].shape
    at = lax.broadcasted_iota(jnp.int32, shape, axis) // size
    odd, high = at % 2 == 1, at // 2 == 1
    one = [None] * 4
    for a, b in ((0, 1), (2, 3)):
        one[a] = jnp.where(odd, pltpu.roll(tiles[b], size, axis), tiles[a])
        one[b] = jnp.where(odd, tiles[b], pltpu.roll(tiles[a], shape[axis] - size, axis))
    two = [None] * 4
    for a, b in ((0, 2), (1, 3)):
        two[a] = jnp.where(high, pltpu.roll(one[b], 2 * size, axis), one[a])
        two[b] = jnp.where(high, one[b], pltpu.roll(one[a], 2 * size, axis))
    return two


def place_channels(x_ref, left_ref):
    for pe in range(8):
        for h in range(2):
            src = pe * 8 + h * 4
            tiles = turn_blocks([x_ref[src + n] for n in range(4)], 1, 32)
            for m4 in range(4):
                rows = slice(16 * pe + 4 * m4, 16 * pe + 4 * m4 + 4)
                for ch in range(2):
                    for part in range(2):
                        cols = slice(256 * part + 128 * h, 256 * part + 128 * h + 128)
                        at = 8 * ch + 4 * part
                        left_ref[ch, rows, cols] = tiles[m4][at : at + 4]


def add_powers(channels, pair, east_ref, chan_ref, residue_ref, prod_ref, acc_ref):
    for ch in channels:
        i = 2 * pair + ch
        sub = chan_ref[16 * i + residue_ref[0]] % 4
        cos = [[east_ref[i, s * 4 + k] for k in range(4)] for s in range(4)]
        sin = [[east_ref[i, 16 + s * 4 + k] for k in range(4)] for s in range(4)]
        for t in range(2):
            for h in range(2):
                total, corr_re, corr_im = None, [None] * 4, [None] * 4
                for p in range(2):
                    re, im = [], []
                    for e in range(4):
                        rows = slice(p * 64 + e * 16 + t * 8, p * 64 + e * 16 + t * 8 + 8)
                        re.append(prod_ref[ch, rows, 128 * h : 128 * h + 128])
                        im.append(prod_ref[ch, rows, 256 + 128 * h : 384 + 128 * h])
                    for e in range(4):
                        square = re[e] * re[e] + im[e] * im[e]
                        total = square if total is None else total + square
                    for k in range(1, 4):
                        for f in range(4 - k):
                            a = re[f + k] * re[f] + im[f + k] * im[f]
                            b = im[f + k] * re[f] - re[f + k] * im[f]
                            corr_re[k] = a if corr_re[k] is None else corr_re[k] + a
                            corr_im[k] = b if corr_im[k] is None else corr_im[k] + b
                for s in range(4):
                    if s == 0:
                        twice = corr_re[1] + corr_re[2] + corr_re[3]
                        power = total + (twice + twice)
                    else:
                        power = total
                        for k in range(1, 4):
                            power = power + (cos[s][k] * corr_re[k] - sin[s][k] * corr_im[k])
                    cols = slice(s * 256 + h * 128, s * 256 + h * 128 + 128)
                    acc_ref[sub, 8 * t : 8 * t + 8, cols] += power


def beam_kernel(
    east_ref, chan_ref, residue_ref, first_ref, odd_ref, next_ref, w_hbm, hot_hbm, out_ref,
    left_ref, prod_ref, acc_ref, w_ref, hot_ref, w_sem, sem
):
    step = pl.program_id(0)
    fetch = pltpu.make_async_copy(hot_hbm, hot_ref, sem)

    def weights(at):
        four = pl.ds(4 * at, 4)
        return pltpu.make_async_copy(w_hbm.at[four], w_ref.at[four], w_sem.at[at])

    block = [pl.when(chan_ref[0] >= 0) for _ in range(4)]

    @pl.when(step == 0)
    def _():
        for at in range(4):
            weights(at).start()
        fetch.start()
        acc_ref[...] = jnp.zeros_like(acc_ref)
        prod_ref[...] = jnp.zeros_like(prod_ref)
        place_channels(first_ref, left_ref.at[0])

    weights(step).wait()

    def multiply(slot):
        for ch in range(2):
            prod_ref[slot, ch] = lax.dot_general(
                left_ref[slot, ch], w_ref[4 * step + 2 * slot + ch], NN, preferred_element_type=F32
            )

    def powers(channel, slot, pair):
        add_powers((channel,), pair, east_ref, chan_ref, residue_ref, prod_ref.at[slot], acc_ref)

    @block[0]
    def _():
        powers(0, 1, jnp.maximum(2 * step - 1, 0))
        multiply(0)

    @block[1]
    def _():
        powers(1, 1, jnp.maximum(2 * step - 1, 0))
        place_channels(odd_ref, left_ref.at[1])

    @block[2]
    def _():
        powers(0, 0, 2 * step)
        multiply(1)

    @block[3]
    def _():
        powers(1, 0, 2 * step)
        place_channels(next_ref, left_ref.at[0])

    @pl.when(step == pl.num_programs(0) - 1)
    def _():
        powers(0, 1, 2 * step + 1)
        powers(1, 1, 2 * step + 1)
        total = acc_ref[...].reshape(64, 1024)
        top = total.astype(BF16)
        rest = (total - top.astype(F32)).astype(BF16)
        parts = jnp.concatenate([top, rest], axis=0)
        fetch.wait()
        out_ref[...] = lax.dot_general(hot_ref[...], parts, NT, preferred_element_type=F32).astype(BF16)


def beams(turned, east, chan_sub, residue, weights, hot):
    smem = pl.BlockSpec(memory_space=pltpu.SMEM)
    return pl.pallas_call(
        beam_kernel,
        name="beams",
        grid=(4,),
        out_shape=jax.ShapeDtypeStruct((1024, 128), BF16),
        in_specs=[
            smem,
            smem,
            smem,
            pl.BlockSpec((64, 16, 128), lambda i: (0, 0, 0)),
            pl.BlockSpec((64, 16, 128), lambda i: (0, 2 * i + 1, 0)),
            pl.BlockSpec((64, 16, 128), lambda i: (0, jnp.minimum(2 * i + 2, 7), 0)),
            pl.BlockSpec(memory_space=pl.ANY),
            pl.BlockSpec(memory_space=pl.ANY),
        ],
        out_specs=pl.BlockSpec((1024, 128), lambda i: (0, 0)),
        scratch_shapes=[
            pltpu.VMEM((2, 2, 128, 512), BF16),
            pltpu.VMEM((2, 2, 128, 512), F32),
            pltpu.VMEM((4, 16, 1024), F32),
            pltpu.VMEM((16, 512, 512), BF16),
            pltpu.VMEM((1024, 1024), BF16),
            pltpu.SemaphoreType.DMA((4,)),
            pltpu.SemaphoreType.DMA,
        ],
        compiler_params=pltpu.CompilerParams(vmem_limit_bytes=51 * MIB),
        cost_estimate=pl.CostEstimate(
            flops=2_000_000_000, bytes_accessed=13_000_000, transcendentals=0
        ),
    )(east, chan_sub, residue.reshape(1), turned, turned, turned, weights, hot)


def weight_kernel(step_ref, out_ref):
    scale = 2 * C * 256
    row = lax.broadcasted_iota(jnp.int32, (16, 256), 0)
    north = lax.broadcasted_iota(jnp.int32, (16, 256), 1)
    for ch in range(2):
        rate = step_ref[2 * pl.program_id(0) + ch]

        def turn(feeds):
            phases = (2.0 * math.pi / scale) * ((rate * (feeds * north)) % scale).astype(F32)
            return jnp.cos(phases), jnp.sin(phases)

        norm = 1.0 / math.sqrt(FEEDS)
        cos, sin = turn(row)
        cos, sin = cos * norm, sin * norm
        more_cos, more_sin = turn(16 + 0 * row)
        for tile in range(16):
            if tile:
                cos, sin = cos * more_cos - sin * more_sin, sin * more_cos + cos * more_sin
            top, low = slice(16 * tile, 16 * tile + 16), slice(256 + 16 * tile, 272 + 16 * tile)
            out_ref[ch, top, 0:256] = cos.astype(BF16)
            out_ref[ch, top, 256:512] = sin.astype(BF16)
            out_ref[ch, low, 0:256] = (-sin).astype(BF16)
            out_ref[ch, low, 256:512] = cos.astype(BF16)


def beam_weights(channels):
    scale = 2 * C
    steps = scale - channels
    weights = pl.pallas_call(
        weight_kernel,
        name="weights",
        grid=(8,),
        out_shape=jax.ShapeDtypeStruct((16, 512, 512), BF16),
        in_specs=[pl.BlockSpec(memory_space=pltpu.SMEM)],
        out_specs=pl.BlockSpec((2, 512, 512), lambda i: (i, 0, 0)),
        compiler_params=pltpu.CompilerParams(vmem_limit_bytes=56 * MIB),
        cost_estimate=pl.CostEstimate(flops=20_000_000, bytes_accessed=6_000_000, transcendentals=500_000),
    )(steps)
    four = jnp.arange(4, dtype=jnp.int32)
    turns = steps[:, None] * (four[:, None] * four[None, :]).reshape(1, 16) % (scale * 4)
    phases = (2.0 * math.pi / (scale * 4)) * turns.astype(F32)
    return weights, 2.0 * jnp.concatenate([jnp.cos(phases), jnp.sin(phases)], axis=1)


def gather_kernel(x_ref, delay_ref, out_ref):
    total = x_ref[0].astype(F32)
    for r in range(1, 16):
        total = total + x_ref[r].astype(F32)
    total = total + pltpu.roll(total, 64, 1)
    top = total.astype(BF16)
    rest = (total - top.astype(F32)).astype(BF16)
    lane = lax.broadcasted_iota(jnp.int32, (64, 128), 1)
    both = jnp.where(lane < 64, top, rest)
    for q in range(4):
        for band in range(4):
            out_ref[4 * q + band, 0:16] = both[16 * q : 16 * q + 16, :]
            out_ref[4 * q + band, 16:24] = delay_ref[band]


def gather_residues(pieces, delays):
    vmem = pl.BlockSpec(memory_space=pltpu.VMEM)
    return pl.pallas_call(
        gather_kernel,
        name="residues",
        out_shape=jax.ShapeDtypeStruct((16, 24, 128), BF16),
        in_specs=[vmem] * 2,
        out_specs=vmem,
        compiler_params=pltpu.CompilerParams(vmem_limit_bytes=4 * MIB),
    )(pieces, delays)


def frame_tables():
    shape = (4, 128, 256)
    band, lane, to = (lax.broadcasted_iota(jnp.int32, shape, axis) for axis in range(3))
    frame = (16 * band + 1 + 4 * (lane % 4) + lane // 4 % 4) % 64
    value = jnp.where(frame == to % 64, 63.0 / 64.0, -1.0 / 64.0) / math.sqrt(C)
    return jnp.where(lane // 16 % 4 == to // 64, value, 0.0).astype(BF16)


def series_kernel(x_ref, tab_ref, out_ref, hot_ref, left_ref):
    series = None
    for band in range(4):
        rows = jnp.concatenate([x_ref[4 * q + band, 0:16] for q in range(4)], axis=0)
        term = lax.dot_general(rows, tab_ref[band], NN, preferred_element_type=F32)
        series = term if series is None else series + term
    ahead = lax.broadcasted_iota(jnp.int32, (64, 128), 0)
    delays = [x_ref[band, 16:24].astype(F32).astype(jnp.int32) for band in range(4)]
    for s in range(16):
        hit = (ahead + delays[s // 4][s % 4 : s % 4 + 1, :]) % 64 == 0
        hot = jnp.where(hit, 1.0, 0.0).astype(BF16)
        for th in range(4):
            cols = slice(128 * th, 128 * th + 128)
            for tile in range(4):
                to = 64 * s + 16 * tile
                at = 16 * ((tile - th) % 4)
                hot_ref[to : to + 16, cols] = hot[at : at + 16, :]
    lane = lax.broadcasted_iota(jnp.int32, (16, 128), 1) % 64
    for at in range(8):
        rows, cols = slice(16 * (at // 2), 16 * (at // 2) + 16), slice(128 * (at % 2), 128 * (at % 2) + 128)
        block = series[rows, cols]
        for t in range(16):
            x = block
            if t:
                x = jnp.where(lane < 64 - t, pltpu.roll(x, 128 - t, 1), pltpu.roll(x, 64 - t, 1))
            top = x.astype(BF16)
            left_ref[0, 16 * t : 16 * t + 16, 128 * at : 128 * at + 128] = top
            left_ref[1, 16 * t : 16 * t + 16, 128 * at : 128 * at + 128] = (x - top.astype(F32)).astype(BF16)
    hot = hot_ref[...]
    out = lax.dot_general(left_ref[0], hot, NN, preferred_element_type=F32)
    out = out + lax.dot_general(left_ref[1], hot, NN, preferred_element_type=F32)
    for th in range(4):
        out_ref[16 * th : 16 * th + 16] = out[:, 128 * th : 128 * th + 128].reshape(16, 16, 128)


def series(sums, tables):
    vmem = pl.BlockSpec(memory_space=pltpu.VMEM)
    return pl.pallas_call(
        series_kernel,
        name="series",
        out_shape=jax.ShapeDtypeStruct((64, 16, 128), F32),
        in_specs=[vmem] * 2,
        out_specs=vmem,
        scratch_shapes=[pltpu.VMEM((1024, 512), BF16), pltpu.VMEM((2, 256, 1024), BF16)],
        compiler_params=pltpu.CompilerParams(vmem_limit_bytes=8 * MIB),
        cost_estimate=pl.CostEstimate(
            flops=600_000_000, bytes_accessed=1_000_000, transcendentals=0
        ),
    )(sums, tables)


def local(voltages, steering, chan_sub, delays):
    groups, band_count = lax.axis_size("grp"), lax.axis_size("band")
    grp_at = lax.axis_index("grp")
    band_at = lax.axis_index("band")
    quarter_at = grp_at % 4
    residue = grp_at // 4

    chunks = spectra(voltages, band_at).reshape(64, 128, 128)
    turned = lax.all_to_all(chunks, "grp", split_axis=0, concat_axis=0, tiled=True)

    place = lambda r, q, b: (4 * r + q) * band_count + b
    swap = [
        (place(r, q, b), place(r, b, q))
        for r in range(groups // 4)
        for q in range(4)
        for b in range(band_count)
    ]
    quarter_subs = lax.ppermute(chan_sub, ("grp", "band"), swap)
    channels = quarter_at * 256 + 16 * jnp.arange(16, dtype=jnp.int32) + residue
    weights, east = beam_weights(channels)
    grid_at = steering[1] * 256 + steering[0]
    hot = (grid_at[:, None] == jnp.arange(1024, dtype=jnp.int32)[None, :]).astype(BF16)
    notes = jnp.transpose(delays.reshape(band_count, 128, 4), (0, 2, 1)).astype(BF16)
    notes = jnp.pad(notes, ((0, 0), (0, 4), (0, 0)))
    sums = beams(turned, east, quarter_subs, residue, weights, hot).reshape(16, 64, 128)
    planes = [[4 * r + q for r in range(groups // 4)] for q in range(4)]
    pieces = lax.all_to_all(
        sums, "grp", split_axis=0, concat_axis=0, tiled=True, axis_index_groups=planes
    )
    columns = [
        [place(r, q, b) for q in range(4) for b in range(band_count)] for r in range(groups // 4)
    ]
    residues = gather_residues(pieces, notes)
    every = lax.all_to_all(
        residues,
        ("grp", "band"),
        split_axis=0,
        concat_axis=0,
        tiled=True,
        axis_index_groups=columns,
    )
    tables = frame_tables()
    return series(every, tables)


def solution(mesh):
    in_specs = (P("band", "grp", None), P(), P("band"), P(None, "band"))
    out_specs = P(None, "grp", "band")
    return jax.shard_map(local, mesh=mesh, in_specs=in_specs, out_specs=out_specs, check_vma=False)
```

```python
import math

import jax
import jax.numpy as jnp
import numpy as np
from jax import lax
from jax.experimental import pallas as pl
from jax.experimental.pallas import tpu as pltpu
from jax.sharding import PartitionSpec as P

A = 2048
FEEDS = 1024
C = 1024
SAMP = 2048
BEAMS = 1024
TRIALS = 512
F32 = jnp.float32
BF16 = jnp.bfloat16
MIB = 1 << 20
NT = (((1,), (1,)), ((), ()))
NN = (((1,), (0,)), ((), ()))


def window_taps():
    tap_pos = np.arange(4 * SAMP) + 0.5
    taper = 0.5 - 0.5 * np.cos(2.0 * np.pi / (4 * SAMP) * tap_pos)
    window = taper * np.sinc((tap_pos - 2 * SAMP) / SAMP)
    window = window * np.sqrt(SAMP / np.sum(window * window))
    return window.reshape(4, SAMP).astype(np.float32)


def lane_tables():
    k = np.arange(64)[:, None]
    lane = np.arange(128)[None, :]

    def rows(r, part):
        angle = 2.0 * np.pi / SAMP * (((16 * k + r) * lane) % SAMP)
        cos, sin = np.cos(angle) / np.sqrt(SAMP), np.sin(angle) / np.sqrt(SAMP)
        if part is not None:
            none = np.zeros_like(cos)
            pair = lambda x: np.concatenate([x, none] if part == 0 else [none, x], axis=1)
            return np.concatenate([pair(cos), pair(-sin)], axis=0)
        sign = -1.0 if r > 8 else 1.0
        top = np.concatenate([cos, -sin * sign], axis=1)
        return np.concatenate([top, np.concatenate([-sin, -cos * sign], axis=1)], axis=0)

    tables = [np.concatenate([rows(0, 0), rows(8, 1)], axis=0)]
    tables += [np.concatenate([rows(at, None), rows(16 - at, None)], axis=0) for at in range(1, 8)]
    return np.stack(tables).astype(jnp.bfloat16)


def real_dft16(x):
    h, c1, c3 = math.sqrt(0.5), math.cos(math.pi / 8), math.cos(3 * math.pi / 8)
    s = [x[j] + x[j + 8] for j in range(8)]
    d = [x[j] - x[j + 8] for j in range(8)]
    ss = [s[j] + s[j + 4] for j in range(4)]
    sd = [s[j] - s[j + 4] for j in range(4)]
    t0, t1 = ss[0] + ss[2], ss[1] + ss[3]
    out = [None] * 9
    out[0] = (t0 + t1, None)
    out[8] = (t0 - t1, None)
    out[4] = (ss[0] - ss[2], ss[1] - ss[3])
    dif, tot = h * (sd[1] - sd[3]), h * (sd[1] + sd[3])
    out[2] = (sd[0] + dif, sd[2] + tot)
    out[6] = (sd[0] - dif, tot - sd[2])
    p = [None] + [d[j] - d[8 - j] for j in (1, 2, 3)]
    q = [None] + [d[j] + d[8 - j] for j in (1, 2, 3)]
    hp, hq = h * p[2], h * q[2]
    ea, eb = d[0] + hp, d[0] - hp
    u, v = c1 * p[1] + c3 * p[3], c3 * p[1] - c1 * p[3]
    fa, fb = d[4] + hq, hq - d[4]
    y, z = c3 * q[1] + c1 * q[3], c1 * q[1] - c3 * q[3]
    out[1] = (ea + u, y + fa)
    out[7] = (ea - u, y - fa)
    out[3] = (eb + v, z + fb)
    out[5] = (eb - v, z - fb)
    return out


def frame_bins(part_ref, win_ref, row0, a0, frame, keep=None):
    lanes = []
    for jb in range(16):
        cols = slice(128 * jb, 128 * jb + 128)
        total = None
        for p in range(4):
            term = frame(p)[pl.ds(a0, 16), cols].astype(F32) * win_ref[p : p + 1, cols]
            if p == 3 and keep is not None:
                total = total * keep
            total = term if total is None else total + term
        lanes.append(total)
    rows = pl.ds(row0, 16)
    for at, (re, im) in enumerate(real_dft16(lanes)):
        if at % 8 == 0:
            part_ref[0, rows, 16 * at : 16 * at + 128] = re.astype(BF16)
        else:
            part_ref[at, rows, 0:128] = re.astype(BF16)
            part_ref[at, rows, 128:256] = im.astype(BF16)


def inner_kernel(v_ref, win_ref, part_ref):
    def body(step, carry):
        m = step // 2
        a0 = pl.multiple_of(16 * (step % 2), 16)
        frame_bins(part_ref, win_ref, pl.multiple_of(16 * step, 16), a0, lambda p: v_ref.at[m - 2 + p])
        return carry

    lax.fori_loop(4, 30, body, 0)


def spectra_kernel(
    band_ref, part_hbm, first_ref, last_ref, prev_ref, next_ref, win_ref, tab_hbm, out_hbm,
    part_ref, tab_ref, stage_ref, turn_ref, in_sem, out_sem
):
    inner = pl.ds(64, 416)
    parts = pltpu.make_async_copy(part_hbm.at[:, inner, :], part_ref.at[:, inner, :], in_sem.at[0])
    tables = pltpu.make_async_copy(tab_hbm, tab_ref, in_sem.at[1])
    for copy in (parts, tables):
        copy.start()
    keep = jnp.where(band_ref[0] == 3, 0.0, 1.0).astype(F32)

    def edge(half, carry):
        a0 = pl.multiple_of(16 * half, 16)
        for m in (0, 1):
            frame = lambda p, m=m: prev_ref.at[m + p] if m + p < 2 else first_ref.at[m + p - 2]
            frame_bins(part_ref, win_ref, pl.multiple_of(32 * m + a0, 16), a0, frame)
        frame = lambda p: last_ref.at[p] if p < 3 else next_ref.at[0]
        frame_bins(part_ref, win_ref, pl.multiple_of(480 + a0, 16), a0, frame, keep)
        return carry

    lax.fori_loop(0, 2, edge, 0)
    parts.wait()
    tables.wait()
    sent = []
    for at in range(8):
        rows = lax.dot_general(tab_ref[at], part_ref[at], NT, preferred_element_type=F32)
        for which in range(2):
            slot = 2 * (at % 2) + which
            for reim in range(2):
                for mb in range(4):
                    r0 = 128 * which + 64 * reim
                    turn_ref[slot, pl.ds(reim * 4 + mb, 64, stride=8), :] = rows[
                        r0 : r0 + 64, 128 * mb : 128 * mb + 128
                    ]
        for which in range(2):
            slot = 2 * (at % 2) + which
            r = at if which == 0 else (8 if at == 0 else 16 - at)
            for q in range(4):
                stage_ref[r, q] = turn_ref[slot, 128 * q : 128 * q + 128, :].astype(BF16)
            copy = pltpu.make_async_copy(stage_ref.at[r], out_hbm.at[r], out_sem.at[r])
            copy.start()
            sent.append(copy)
    for copy in sent:
        copy.wait()


def spectra(voltages, band_at):
    band_count = lax.axis_size("band")
    ahead = lax.ppermute(voltages[14:16], "band", [(i, i + 1) for i in range(band_count - 1)])
    behind = lax.ppermute(voltages[0:1], "band", [(i, (i - 1) % band_count) for i in range(band_count)])
    window, tables = jnp.asarray(window_taps()), jnp.asarray(lane_tables())
    vmem, smem = pl.BlockSpec(memory_space=pltpu.VMEM), pl.BlockSpec(memory_space=pltpu.SMEM)
    anywhere = pl.BlockSpec(memory_space=pl.ANY)
    parts = pl.pallas_call(
        inner_kernel,
        name="inner_frames",
        out_shape=jax.ShapeDtypeStruct((8, 512, 256), BF16),
        in_specs=[vmem] * 2,
        out_specs=vmem,
        compiler_params=pltpu.CompilerParams(vmem_limit_bytes=58 * MIB),
        cost_estimate=pl.CostEstimate(flops=20_000_000, bytes_accessed=4_000_000, transcendentals=0),
    )(voltages, window)
    return pl.pallas_call(
        spectra_kernel,
        name="spectra",
        out_shape=jax.ShapeDtypeStruct((16, 4, 128, 128), BF16),
        in_specs=[smem, anywhere, vmem, vmem, vmem, vmem, vmem, anywhere],
        out_specs=pl.BlockSpec(memory_space=pltpu.HBM),
        scratch_shapes=[
            pltpu.VMEM((8, 512, 256), BF16),
            pltpu.VMEM((8, 256, 256), BF16),
            pltpu.VMEM((16, 4, 128, 128), BF16),
            pltpu.VMEM((4, 512, 128), F32),
            pltpu.SemaphoreType.DMA((2,)),
            pltpu.SemaphoreType.DMA((16,)),
        ],
        compiler_params=pltpu.CompilerParams(vmem_limit_bytes=52 * MIB),
        cost_estimate=pl.CostEstimate(
            flops=600_000_000, bytes_accessed=6_000_000, transcendentals=0
        ),
    )(band_at.reshape(1), parts, voltages[0:3], voltages[13:16], ahead, behind, window, tables)


def turn_blocks(tiles, axis, size):
    shape = tiles[0].shape
    at = lax.broadcasted_iota(jnp.int32, shape, axis) // size
    odd, high = at % 2 == 1, at // 2 == 1
    one = [None] * 4
    for a, b in ((0, 1), (2, 3)):
        one[a] = jnp.where(odd, pltpu.roll(tiles[b], size, axis), tiles[a])
        one[b] = jnp.where(odd, tiles[b], pltpu.roll(tiles[a], shape[axis] - size, axis))
    two = [None] * 4
    for a, b in ((0, 2), (1, 3)):
        two[a] = jnp.where(high, pltpu.roll(one[b], 2 * size, axis), one[a])
        two[b] = jnp.where(high, one[b], pltpu.roll(one[a], 2 * size, axis))
    return two


def place_channels(x_ref, left_ref):
    for pe in range(8):
        for h in range(2):
            src = pe * 8 + h * 4
            tiles = turn_blocks([x_ref[src + n] for n in range(4)], 1, 32)
            for m4 in range(4):
                rows = slice(16 * pe + 4 * m4, 16 * pe + 4 * m4 + 4)
                for ch in range(2):
                    for part in range(2):
                        cols = slice(256 * part + 128 * h, 256 * part + 128 * h + 128)
                        at = 8 * ch + 4 * part
                        left_ref[ch, rows, cols] = tiles[m4][at : at + 4]


def add_powers(channels, pair, east_ref, chan_ref, residue_ref, prod_ref, acc_ref):
    for ch in channels:
        i = 2 * pair + ch
        sub = chan_ref[16 * i + residue_ref[0]] % 4
        cos = [[east_ref[i, s * 4 + k] for k in range(4)] for s in range(4)]
        sin = [[east_ref[i, 16 + s * 4 + k] for k in range(4)] for s in range(4)]
        for t in range(2):
            for h in range(2):
                total, corr_re, corr_im = None, [None] * 4, [None] * 4
                for p in range(2):
                    re, im = [], []
                    for e in range(4):
                        rows = slice(p * 64 + e * 16 + t * 8, p * 64 + e * 16 + t * 8 + 8)
                        re.append(prod_ref[ch, rows, 128 * h : 128 * h + 128])
                        im.append(prod_ref[ch, rows, 256 + 128 * h : 384 + 128 * h])
                    for e in range(4):
                        square = re[e] * re[e] + im[e] * im[e]
                        total = square if total is None else total + square
                    for k in range(1, 4):
                        for f in range(4 - k):
                            a = re[f + k] * re[f] + im[f + k] * im[f]
                            b = im[f + k] * re[f] - re[f + k] * im[f]
                            corr_re[k] = a if corr_re[k] is None else corr_re[k] + a
                            corr_im[k] = b if corr_im[k] is None else corr_im[k] + b
                for s in range(4):
                    if s == 0:
                        twice = corr_re[1] + corr_re[2] + corr_re[3]
                        power = total + (twice + twice)
                    else:
                        power = total
                        for k in range(1, 4):
                            power = power + (cos[s][k] * corr_re[k] - sin[s][k] * corr_im[k])
                    cols = slice(s * 256 + h * 128, s * 256 + h * 128 + 128)
                    acc_ref[sub, 8 * t : 8 * t + 8, cols] += power


def beam_kernel(
    east_ref, chan_ref, residue_ref, first_ref, odd_ref, next_ref, w_hbm, hot_hbm, out_ref,
    left_ref, prod_ref, acc_ref, w_ref, hot_ref, w_sem, sem
):
    step = pl.program_id(0)
    fetch = pltpu.make_async_copy(hot_hbm, hot_ref, sem)

    def weights(at):
        four = pl.ds(4 * at, 4)
        return pltpu.make_async_copy(w_hbm.at[four], w_ref.at[four], w_sem.at[at])

    block = [pl.when(chan_ref[0] >= 0) for at in range(4)]

    @pl.when(step == 0)
    def _():
        for at in range(4):
            weights(at).start()
        fetch.start()
        acc_ref[...] = jnp.zeros_like(acc_ref)
        prod_ref[...] = jnp.zeros_like(prod_ref)
        place_channels(first_ref, left_ref.at[0])

    weights(step).wait()

    def multiply(slot):
        for ch in range(2):
            prod_ref[slot, ch] = lax.dot_general(
                left_ref[slot, ch], w_ref[4 * step + 2 * slot + ch], NN, preferred_element_type=F32
            )

    def powers(channel, slot, pair):
        add_powers((channel,), pair, east_ref, chan_ref, residue_ref, prod_ref.at[slot], acc_ref)

    @block[0]
    def _():
        powers(0, 1, jnp.maximum(2 * step - 1, 0))
        multiply(0)

    @block[1]
    def _():
        powers(1, 1, jnp.maximum(2 * step - 1, 0))
        place_channels(odd_ref, left_ref.at[1])

    @block[2]
    def _():
        powers(0, 0, 2 * step)
        multiply(1)

    @block[3]
    def _():
        powers(1, 0, 2 * step)
        place_channels(next_ref, left_ref.at[0])

    @pl.when(step == pl.num_programs(0) - 1)
    def _():
        powers(0, 1, 2 * step + 1)
        powers(1, 1, 2 * step + 1)
        total = acc_ref[...].reshape(64, 1024)
        top = total.astype(BF16)
        rest = (total - top.astype(F32)).astype(BF16)
        parts = jnp.concatenate([top, rest], axis=0)
        fetch.wait()
        out_ref[...] = lax.dot_general(hot_ref[...], parts, NT, preferred_element_type=F32).astype(BF16)


def beams(turned, east, chan_sub, residue, weights, hot):
    smem = pl.BlockSpec(memory_space=pltpu.SMEM)
    return pl.pallas_call(
        beam_kernel,
        name="beams",
        grid=(4,),
        out_shape=jax.ShapeDtypeStruct((1024, 128), BF16),
        in_specs=[
            smem,
            smem,
            smem,
            pl.BlockSpec((64, 16, 128), lambda i: (0, 0, 0)),
            pl.BlockSpec((64, 16, 128), lambda i: (0, 2 * i + 1, 0)),
            pl.BlockSpec((64, 16, 128), lambda i: (0, jnp.minimum(2 * i + 2, 7), 0)),
            pl.BlockSpec(memory_space=pl.ANY),
            pl.BlockSpec(memory_space=pl.ANY),
        ],
        out_specs=pl.BlockSpec((1024, 128), lambda i: (0, 0)),
        scratch_shapes=[
            pltpu.VMEM((2, 2, 128, 512), BF16),
            pltpu.VMEM((2, 2, 128, 512), F32),
            pltpu.VMEM((4, 16, 1024), F32),
            pltpu.VMEM((16, 512, 512), BF16),
            pltpu.VMEM((1024, 1024), BF16),
            pltpu.SemaphoreType.DMA((4,)),
            pltpu.SemaphoreType.DMA,
        ],
        compiler_params=pltpu.CompilerParams(vmem_limit_bytes=51 * MIB),
        cost_estimate=pl.CostEstimate(
            flops=2_000_000_000, bytes_accessed=13_000_000, transcendentals=0
        ),
    )(east, chan_sub, residue.reshape(1), turned, turned, turned, weights, hot)


def weight_kernel(step_ref, out_ref):
    scale = 2 * C * 256
    row = lax.broadcasted_iota(jnp.int32, (16, 256), 0)
    north = lax.broadcasted_iota(jnp.int32, (16, 256), 1)
    for ch in range(2):
        rate = step_ref[2 * pl.program_id(0) + ch]

        def turn(feeds):
            phases = (2.0 * math.pi / scale) * ((rate * (feeds * north)) % scale).astype(F32)
            return jnp.cos(phases), jnp.sin(phases)

        norm = 1.0 / math.sqrt(FEEDS)
        cos, sin = turn(row)
        cos, sin = cos * norm, sin * norm
        more_cos, more_sin = turn(16 + 0 * row)
        for tile in range(16):
            if tile:
                cos, sin = cos * more_cos - sin * more_sin, sin * more_cos + cos * more_sin
            top, low = slice(16 * tile, 16 * tile + 16), slice(256 + 16 * tile, 272 + 16 * tile)
            out_ref[ch, top, 0:256] = cos.astype(BF16)
            out_ref[ch, top, 256:512] = sin.astype(BF16)
            out_ref[ch, low, 0:256] = (-sin).astype(BF16)
            out_ref[ch, low, 256:512] = cos.astype(BF16)


def beam_weights(channels):
    scale = 2 * C
    steps = scale - channels
    weights = pl.pallas_call(
        weight_kernel,
        name="weights",
        grid=(8,),
        out_shape=jax.ShapeDtypeStruct((16, 512, 512), BF16),
        in_specs=[pl.BlockSpec(memory_space=pltpu.SMEM)],
        out_specs=pl.BlockSpec((2, 512, 512), lambda i: (i, 0, 0)),
        compiler_params=pltpu.CompilerParams(vmem_limit_bytes=56 * MIB),
        cost_estimate=pl.CostEstimate(flops=20_000_000, bytes_accessed=6_000_000, transcendentals=500_000),
    )(steps)
    four = jnp.arange(4, dtype=jnp.int32)
    turns = steps[:, None] * (four[:, None] * four[None, :]).reshape(1, 16) % (scale * 4)
    phases = (2.0 * math.pi / (scale * 4)) * turns.astype(F32)
    return weights, 2.0 * jnp.concatenate([jnp.cos(phases), jnp.sin(phases)], axis=1)


def gather_kernel(x_ref, delay_ref, out_ref):
    total = x_ref[0].astype(F32)
    for r in range(1, 16):
        total = total + x_ref[r].astype(F32)
    total = total + pltpu.roll(total, 64, 1)
    top = total.astype(BF16)
    rest = (total - top.astype(F32)).astype(BF16)
    lane = lax.broadcasted_iota(jnp.int32, (64, 128), 1)
    both = jnp.where(lane < 64, top, rest)
    for q in range(4):
        for band in range(4):
            out_ref[4 * q + band, 0:16] = both[16 * q : 16 * q + 16, :]
            out_ref[4 * q + band, 16:24] = delay_ref[band]


def gather_residues(pieces, delays):
    vmem = pl.BlockSpec(memory_space=pltpu.VMEM)
    return pl.pallas_call(
        gather_kernel,
        name="residues",
        out_shape=jax.ShapeDtypeStruct((16, 24, 128), BF16),
        in_specs=[vmem] * 2,
        out_specs=vmem,
        compiler_params=pltpu.CompilerParams(vmem_limit_bytes=4 * MIB),
    )(pieces, delays)


def frame_tables():
    table = np.zeros((4, 2, 4, 4, 4, 4, 64), np.float32)
    for band in range(4):
        for m4 in range(4):
            for mb in range(4):
                row = np.full(64, -1.0 / 64.0)
                row[(16 * band + 1 + 4 * mb + m4) % 64] += 1.0
                for sub in range(4):
                    table[band, :, sub, m4, mb, sub, :] = row / math.sqrt(C)
    return table.reshape(4, 128, 256).astype(jnp.bfloat16)


def series_kernel(x_ref, tab_ref, out_ref, hot_ref, left_ref):
    series = None
    for band in range(4):
        rows = jnp.concatenate([x_ref[4 * q + band, 0:16] for q in range(4)], axis=0)
        term = lax.dot_general(rows, tab_ref[band], NN, preferred_element_type=F32)
        series = term if series is None else series + term
    ahead = lax.broadcasted_iota(jnp.int32, (64, 128), 0)
    delays = [x_ref[band, 16:24].astype(F32).astype(jnp.int32) for band in range(4)]
    for s in range(16):
        hit = (ahead + delays[s // 4][s % 4 : s % 4 + 1, :]) % 64 == 0
        hot = jnp.where(hit, 1.0, 0.0).astype(BF16)
        for th in range(4):
            cols = slice(128 * th, 128 * th + 128)
            for tile in range(4):
                to = 64 * s + 16 * tile
                at = 16 * ((tile - th) % 4)
                hot_ref[to : to + 16, cols] = hot[at : at + 16, :]
    lane = lax.broadcasted_iota(jnp.int32, (16, 128), 1) % 64
    for at in range(8):
        rows, cols = slice(16 * (at // 2), 16 * (at // 2) + 16), slice(128 * (at % 2), 128 * (at % 2) + 128)
        block = series[rows, cols]
        for t in range(16):
            x = block
            if t:
                x = jnp.where(lane < 64 - t, pltpu.roll(x, 128 - t, 1), pltpu.roll(x, 64 - t, 1))
            top = x.astype(BF16)
            left_ref[0, 16 * t : 16 * t + 16, 128 * at : 128 * at + 128] = top
            left_ref[1, 16 * t : 16 * t + 16, 128 * at : 128 * at + 128] = (x - top.astype(F32)).astype(BF16)
    hot = hot_ref[...]
    out = lax.dot_general(left_ref[0], hot, NN, preferred_element_type=F32)
    out = out + lax.dot_general(left_ref[1], hot, NN, preferred_element_type=F32)
    for th in range(4):
        out_ref[16 * th : 16 * th + 16] = out[:, 128 * th : 128 * th + 128].reshape(16, 16, 128)


def series(sums):
    vmem = pl.BlockSpec(memory_space=pltpu.VMEM)
    return pl.pallas_call(
        series_kernel,
        name="series",
        out_shape=jax.ShapeDtypeStruct((64, 16, 128), F32),
        in_specs=[vmem] * 2,
        out_specs=vmem,
        scratch_shapes=[pltpu.VMEM((1024, 512), BF16), pltpu.VMEM((2, 256, 1024), BF16)],
        compiler_params=pltpu.CompilerParams(vmem_limit_bytes=8 * MIB),
        cost_estimate=pl.CostEstimate(
            flops=600_000_000, bytes_accessed=1_000_000, transcendentals=0
        ),
    )(sums, jnp.asarray(frame_tables()))


def local(voltages, steering, chan_sub, delays):
    groups, band_count = lax.axis_size("grp"), lax.axis_size("band")
    grp_at = lax.axis_index("grp")
    band_at = lax.axis_index("band")
    quarter_at = grp_at % 4
    residue = grp_at // 4

    chunks = spectra(voltages, band_at).reshape(64, 128, 128)
    turned = lax.all_to_all(chunks, "grp", split_axis=0, concat_axis=0, tiled=True)

    place = lambda r, q, b: (4 * r + q) * band_count + b
    swap = [
        (place(r, q, b), place(r, b, q))
        for r in range(groups // 4)
        for q in range(4)
        for b in range(band_count)
    ]
    quarter_subs = lax.ppermute(chan_sub, ("grp", "band"), swap)
    channels = quarter_at * 256 + 16 * jnp.arange(16, dtype=jnp.int32) + residue
    weights, east = beam_weights(channels)
    grid_at = steering[1] * 256 + steering[0]
    hot = (grid_at[:, None] == jnp.arange(1024, dtype=jnp.int32)[None, :]).astype(BF16)
    notes = jnp.transpose(delays.reshape(band_count, 128, 4), (0, 2, 1)).astype(BF16)
    notes = jnp.pad(notes, ((0, 0), (0, 4), (0, 0)))
    sums = beams(turned, east, quarter_subs, residue, weights, hot).reshape(16, 64, 128)
    planes = [[4 * r + q for r in range(groups // 4)] for q in range(4)]
    pieces = lax.all_to_all(
        sums, "grp", split_axis=0, concat_axis=0, tiled=True, axis_index_groups=planes
    )
    columns = [
        [place(r, q, b) for q in range(4) for b in range(band_count)] for r in range(groups // 4)
    ]
    every = lax.all_to_all(
        gather_residues(pieces, notes),
        ("grp", "band"),
        split_axis=0,
        concat_axis=0,
        tiled=True,
        axis_index_groups=columns,
    )
    return series(every)


def solution(mesh):
    in_specs = (P("band", "grp", None), P(), P("band"), P(None, "band"))
    out_specs = P(None, "grp", "band")
    return jax.shard_map(local, mesh=mesh, in_specs=in_specs, out_specs=out_specs, check_vma=False)
```

```python
import math

import jax
import jax.numpy as jnp
import numpy as np
from jax import lax
from jax.experimental import pallas as pl
from jax.experimental.pallas import tpu as pltpu
from jax.sharding import PartitionSpec as P

A = 2048
FEEDS = 1024
C = 1024
SAMP = 2048
BEAMS = 1024
TRIALS = 512
F32 = jnp.float32
BF16 = jnp.bfloat16
MIB = 1 << 20
NT = (((1,), (1,)), ((), ()))
NN = (((1,), (0,)), ((), ()))


def window_taps():
    tap_pos = np.arange(4 * SAMP) + 0.5
    taper = 0.5 - 0.5 * np.cos(2.0 * np.pi / (4 * SAMP) * tap_pos)
    window = taper * np.sinc((tap_pos - 2 * SAMP) / SAMP)
    window = window * np.sqrt(SAMP / np.sum(window * window))
    return window.reshape(4, SAMP).astype(np.float32)


def lane_tables():
    k = np.arange(64)[:, None]
    lane = np.arange(128)[None, :]

    def rows(r, part):
        angle = 2.0 * np.pi / SAMP * (((16 * k + r) * lane) % SAMP)
        cos, sin = np.cos(angle) / np.sqrt(SAMP), np.sin(angle) / np.sqrt(SAMP)
        if part is not None:
            none = np.zeros_like(cos)
            pair = lambda x: np.concatenate([x, none] if part == 0 else [none, x], axis=1)
            return np.concatenate([pair(cos), pair(-sin)], axis=0)
        sign = -1.0 if r > 8 else 1.0
        top = np.concatenate([cos, -sin * sign], axis=1)
        return np.concatenate([top, np.concatenate([-sin, -cos * sign], axis=1)], axis=0)

    tables = [np.concatenate([rows(0, 0), rows(8, 1)], axis=0)]
    tables += [np.concatenate([rows(at, None), rows(16 - at, None)], axis=0) for at in range(1, 8)]
    return np.stack(tables).astype(jnp.bfloat16)


def real_dft16(x):
    h, c1, c3 = math.sqrt(0.5), math.cos(math.pi / 8), math.cos(3 * math.pi / 8)
    s = [x[j] + x[j + 8] for j in range(8)]
    d = [x[j] - x[j + 8] for j in range(8)]
    ss = [s[j] + s[j + 4] for j in range(4)]
    sd = [s[j] - s[j + 4] for j in range(4)]
    t0, t1 = ss[0] + ss[2], ss[1] + ss[3]
    out = [None] * 9
    out[0] = (t0 + t1, None)
    out[8] = (t0 - t1, None)
    out[4] = (ss[0] - ss[2], ss[1] - ss[3])
    dif, tot = h * (sd[1] - sd[3]), h * (sd[1] + sd[3])
    out[2] = (sd[0] + dif, sd[2] + tot)
    out[6] = (sd[0] - dif, tot - sd[2])
    p = [None] + [d[j] - d[8 - j] for j in (1, 2, 3)]
    q = [None] + [d[j] + d[8 - j] for j in (1, 2, 3)]
    hp, hq = h * p[2], h * q[2]
    ea, eb = d[0] + hp, d[0] - hp
    u, v = c1 * p[1] + c3 * p[3], c3 * p[1] - c1 * p[3]
    fa, fb = d[4] + hq, hq - d[4]
    y, z = c3 * q[1] + c1 * q[3], c1 * q[1] - c3 * q[3]
    out[1] = (ea + u, y + fa)
    out[7] = (ea - u, y - fa)
    out[3] = (eb + v, z + fb)
    out[5] = (eb - v, z - fb)
    return out


def frame_bins(part_ref, win_ref, row0, a0, frame, keep=None):
    lanes = []
    for jb in range(16):
        cols = slice(128 * jb, 128 * jb + 128)
        total = None
        for p in range(4):
            term = frame(p)[pl.ds(a0, 16), cols].astype(F32) * win_ref[p : p + 1, cols]
            if p == 3 and keep is not None:
                total = total * keep
            total = term if total is None else total + term
        lanes.append(total)
    rows = pl.ds(row0, 16)
    for at, (re, im) in enumerate(real_dft16(lanes)):
        if at % 8 == 0:
            part_ref[0, rows, 16 * at : 16 * at + 128] = re.astype(BF16)
        else:
            part_ref[at, rows, 0:128] = re.astype(BF16)
            part_ref[at, rows, 128:256] = im.astype(BF16)


def inner_kernel(v_ref, win_ref, part_ref):
    def body(step, carry):
        m = step // 2
        a0 = pl.multiple_of(16 * (step % 2), 16)
        frame_bins(part_ref, win_ref, pl.multiple_of(16 * step, 16), a0, lambda p: v_ref.at[m - 2 + p])
        return carry

    lax.fori_loop(4, 30, body, 0)


def spectra_kernel(
    band_ref, part_hbm, first_ref, last_ref, prev_ref, next_ref, win_ref, tab_hbm, out_hbm,
    part_ref, tab_ref, stage_ref, turn_ref, in_sem, out_sem
):
    inner = pl.ds(64, 416)
    parts = pltpu.make_async_copy(part_hbm.at[:, inner, :], part_ref.at[:, inner, :], in_sem.at[0])
    tables = pltpu.make_async_copy(tab_hbm, tab_ref, in_sem.at[1])
    for copy in (parts, tables):
        copy.start()
    keep = jnp.where(band_ref[0] == 3, 0.0, 1.0).astype(F32)

    def edge(half, carry):
        a0 = pl.multiple_of(16 * half, 16)
        for m in (0, 1):
            frame = lambda p, m=m: prev_ref.at[m + p] if m + p < 2 else first_ref.at[m + p - 2]
            frame_bins(part_ref, win_ref, pl.multiple_of(32 * m + a0, 16), a0, frame)
        frame = lambda p: last_ref.at[p] if p < 3 else next_ref.at[0]
        frame_bins(part_ref, win_ref, pl.multiple_of(480 + a0, 16), a0, frame, keep)
        return carry

    lax.fori_loop(0, 2, edge, 0)
    parts.wait()
    tables.wait()
    sent = []
    for at in range(8):
        rows = lax.dot_general(tab_ref[at], part_ref[at], NT, preferred_element_type=F32)
        for which in range(2):
            slot = 2 * (at % 2) + which
            for reim in range(2):
                for mb in range(4):
                    r0 = 128 * which + 64 * reim
                    turn_ref[slot, pl.ds(reim * 4 + mb, 64, stride=8), :] = rows[
                        r0 : r0 + 64, 128 * mb : 128 * mb + 128
                    ]
        for which in range(2):
            slot = 2 * (at % 2) + which
            r = at if which == 0 else (8 if at == 0 else 16 - at)
            for q in range(4):
                stage_ref[r, q] = turn_ref[slot, 128 * q : 128 * q + 128, :].astype(BF16)
            copy = pltpu.make_async_copy(stage_ref.at[r], out_hbm.at[r], out_sem.at[r])
            copy.start()
            sent.append(copy)
    for copy in sent:
        copy.wait()


def spectra(voltages, band_at):
    band_count = lax.axis_size("band")
    ahead = lax.ppermute(voltages[14:16], "band", [(i, i + 1) for i in range(band_count - 1)])
    behind = lax.ppermute(voltages[0:1], "band", [(i, (i - 1) % band_count) for i in range(band_count)])
    window, tables = jnp.asarray(window_taps()), jnp.asarray(lane_tables())
    vmem, smem = pl.BlockSpec(memory_space=pltpu.VMEM), pl.BlockSpec(memory_space=pltpu.SMEM)
    anywhere = pl.BlockSpec(memory_space=pl.ANY)
    parts = pl.pallas_call(
        inner_kernel,
        name="inner_frames",
        out_shape=jax.ShapeDtypeStruct((8, 512, 256), BF16),
        in_specs=[vmem] * 2,
        out_specs=vmem,
        compiler_params=pltpu.CompilerParams(vmem_limit_bytes=58 * MIB),
        cost_estimate=pl.CostEstimate(flops=20_000_000, bytes_accessed=4_000_000, transcendentals=0),
    )(voltages, window)
    return pl.pallas_call(
        spectra_kernel,
        name="spectra",
        out_shape=jax.ShapeDtypeStruct((16, 4, 128, 128), BF16),
        in_specs=[smem, anywhere, vmem, vmem, vmem, vmem, vmem, anywhere],
        out_specs=pl.BlockSpec(memory_space=pltpu.HBM),
        scratch_shapes=[
            pltpu.VMEM((8, 512, 256), BF16),
            pltpu.VMEM((8, 256, 256), BF16),
            pltpu.VMEM((16, 4, 128, 128), BF16),
            pltpu.VMEM((4, 512, 128), F32),
            pltpu.SemaphoreType.DMA((2,)),
            pltpu.SemaphoreType.DMA((16,)),
        ],
        compiler_params=pltpu.CompilerParams(vmem_limit_bytes=52 * MIB),
        cost_estimate=pl.CostEstimate(
            flops=600_000_000, bytes_accessed=6_000_000, transcendentals=0
        ),
    )(band_at.reshape(1), parts, voltages[0:3], voltages[13:16], ahead, behind, window, tables)


def turn_blocks(tiles, axis, size):
    shape = tiles[0].shape
    at = lax.broadcasted_iota(jnp.int32, shape, axis) // size
    odd, high = at % 2 == 1, at // 2 == 1
    one = [None] * 4
    for a, b in ((0, 1), (2, 3)):
        one[a] = jnp.where(odd, pltpu.roll(tiles[b], size, axis), tiles[a])
        one[b] = jnp.where(odd, tiles[b], pltpu.roll(tiles[a], shape[axis] - size, axis))
    two = [None] * 4
    for a, b in ((0, 2), (1, 3)):
        two[a] = jnp.where(high, pltpu.roll(one[b], 2 * size, axis), one[a])
        two[b] = jnp.where(high, one[b], pltpu.roll(one[a], 2 * size, axis))
    return two


def place_channels(x_ref, left_ref):
    for pe in range(8):
        for h in range(2):
            src = pe * 8 + h * 4
            tiles = turn_blocks([x_ref[src + n] for n in range(4)], 1, 32)
            for m4 in range(4):
                rows = slice(16 * pe + 4 * m4, 16 * pe + 4 * m4 + 4)
                for ch in range(2):
                    for part in range(2):
                        cols = slice(256 * part + 128 * h, 256 * part + 128 * h + 128)
                        at = 8 * ch + 4 * part
                        left_ref[ch, rows, cols] = tiles[m4][at : at + 4]


def add_powers(channels, pair, east_ref, chan_ref, residue_ref, prod_ref, acc_ref):
    for ch in channels:
        i = 2 * pair + ch
        sub = chan_ref[16 * i + residue_ref[0]] % 4
        cos = [[east_ref[i, s * 4 + k] for k in range(4)] for s in range(4)]
        sin = [[east_ref[i, 16 + s * 4 + k] for k in range(4)] for s in range(4)]
        for t in range(2):
            for h in range(2):
                total, corr_re, corr_im = None, [None] * 4, [None] * 4
                for p in range(2):
                    re, im = [], []
                    for e in range(4):
                        rows = slice(p * 64 + e * 16 + t * 8, p * 64 + e * 16 + t * 8 + 8)
                        re.append(prod_ref[ch, rows, 128 * h : 128 * h + 128])
                        im.append(prod_ref[ch, rows, 256 + 128 * h : 384 + 128 * h])
                    for e in range(4):
                        square = re[e] * re[e] + im[e] * im[e]
                        total = square if total is None else total + square
                    for k in range(1, 4):
                        for f in range(4 - k):
                            a = re[f + k] * re[f] + im[f + k] * im[f]
                            b = im[f + k] * re[f] - re[f + k] * im[f]
                            corr_re[k] = a if corr_re[k] is None else corr_re[k] + a
                            corr_im[k] = b if corr_im[k] is None else corr_im[k] + b
                for s in range(4):
                    if s == 0:
                        twice = corr_re[1] + corr_re[2] + corr_re[3]
                        power = total + (twice + twice)
                    else:
                        power = total
                        for k in range(1, 4):
                            power = power + (cos[s][k] * corr_re[k] - sin[s][k] * corr_im[k])
                    cols = slice(s * 256 + h * 128, s * 256 + h * 128 + 128)
                    acc_ref[sub, 8 * t : 8 * t + 8, cols] += power


def beam_kernel(
    east_ref, chan_ref, residue_ref, first_ref, odd_ref, next_ref, w_hbm, hot_hbm, out_ref,
    left_ref, prod_ref, acc_ref, w_ref, hot_ref, w_sem, sem
):
    step = pl.program_id(0)
    fetch = pltpu.make_async_copy(hot_hbm, hot_ref, sem)

    def weights(at):
        four = pl.ds(4 * at, 4)
        return pltpu.make_async_copy(w_hbm.at[four], w_ref.at[four], w_sem.at[at])

    block = [pl.when(chan_ref[0] >= 0) for at in range(4)]

    @pl.when(step == 0)
    def _():
        for at in range(4):
            weights(at).start()
        fetch.start()
        acc_ref[...] = jnp.zeros_like(acc_ref)
        prod_ref[...] = jnp.zeros_like(prod_ref)
        place_channels(first_ref, left_ref.at[0])

    weights(step).wait()

    def multiply(slot):
        for ch in range(2):
            prod_ref[slot, ch] = lax.dot_general(
                left_ref[slot, ch], w_ref[4 * step + 2 * slot + ch], NN, preferred_element_type=F32
            )

    def powers(channel, slot, pair):
        add_powers((channel,), pair, east_ref, chan_ref, residue_ref, prod_ref.at[slot], acc_ref)

    @block[0]
    def _():
        powers(0, 1, jnp.maximum(2 * step - 1, 0))
        multiply(0)

    @block[1]
    def _():
        powers(1, 1, jnp.maximum(2 * step - 1, 0))
        place_channels(odd_ref, left_ref.at[1])

    @block[2]
    def _():
        powers(0, 0, 2 * step)
        multiply(1)

    @block[3]
    def _():
        powers(1, 0, 2 * step)
        place_channels(next_ref, left_ref.at[0])

    @pl.when(step == pl.num_programs(0) - 1)
    def _():
        powers(0, 1, 2 * step + 1)
        powers(1, 1, 2 * step + 1)
        total = acc_ref[...].reshape(64, 1024)
        top = total.astype(BF16)
        rest = (total - top.astype(F32)).astype(BF16)
        parts = jnp.concatenate([top, rest], axis=0)
        fetch.wait()
        out_ref[...] = lax.dot_general(hot_ref[...], parts, NT, preferred_element_type=F32).astype(BF16)


def beams(turned, east, chan_sub, residue, weights, hot):
    smem = pl.BlockSpec(memory_space=pltpu.SMEM)
    return pl.pallas_call(
        beam_kernel,
        name="beams",
        grid=(4,),
        out_shape=jax.ShapeDtypeStruct((1024, 128), BF16),
        in_specs=[
            smem,
            smem,
            smem,
            pl.BlockSpec((64, 16, 128), lambda i: (0, 0, 0)),
            pl.BlockSpec((64, 16, 128), lambda i: (0, 2 * i + 1, 0)),
            pl.BlockSpec((64, 16, 128), lambda i: (0, jnp.minimum(2 * i + 2, 7), 0)),
            pl.BlockSpec(memory_space=pl.ANY),
            pl.BlockSpec(memory_space=pl.ANY),
        ],
        out_specs=pl.BlockSpec((1024, 128), lambda i: (0, 0)),
        scratch_shapes=[
            pltpu.VMEM((2, 2, 128, 512), BF16),
            pltpu.VMEM((2, 2, 128, 512), F32),
            pltpu.VMEM((4, 16, 1024), F32),
            pltpu.VMEM((16, 512, 512), BF16),
            pltpu.VMEM((1024, 1024), BF16),
            pltpu.SemaphoreType.DMA((4,)),
            pltpu.SemaphoreType.DMA,
        ],
        compiler_params=pltpu.CompilerParams(vmem_limit_bytes=51 * MIB),
        cost_estimate=pl.CostEstimate(
            flops=2_000_000_000, bytes_accessed=13_000_000, transcendentals=0
        ),
    )(east, chan_sub, residue.reshape(1), turned, turned, turned, weights, hot)


def weight_kernel(step_ref, out_ref):
    scale = 2 * C * 256
    row = lax.broadcasted_iota(jnp.int32, (16, 256), 0)
    north = lax.broadcasted_iota(jnp.int32, (16, 256), 1)
    for ch in range(2):
        rate = step_ref[2 * pl.program_id(0) + ch]

        def turn(feeds):
            phases = (2.0 * math.pi / scale) * ((rate * (feeds * north)) % scale).astype(F32)
            return jnp.cos(phases), jnp.sin(phases)

        norm = 1.0 / math.sqrt(FEEDS)
        cos, sin = turn(row)
        cos, sin = cos * norm, sin * norm
        more_cos, more_sin = turn(16 + 0 * row)
        for tile in range(16):
            if tile:
                cos, sin = cos * more_cos - sin * more_sin, sin * more_cos + cos * more_sin
            top, low = slice(16 * tile, 16 * tile + 16), slice(256 + 16 * tile, 272 + 16 * tile)
            out_ref[ch, top, 0:256] = cos.astype(BF16)
            out_ref[ch, top, 256:512] = sin.astype(BF16)
            out_ref[ch, low, 0:256] = (-sin).astype(BF16)
            out_ref[ch, low, 256:512] = cos.astype(BF16)


def beam_weights(channels):
    scale = 2 * C
    steps = scale - channels
    weights = pl.pallas_call(
        weight_kernel,
        name="weights",
        grid=(8,),
        out_shape=jax.ShapeDtypeStruct((16, 512, 512), BF16),
        in_specs=[pl.BlockSpec(memory_space=pltpu.SMEM)],
        out_specs=pl.BlockSpec((2, 512, 512), lambda i: (i, 0, 0)),
        compiler_params=pltpu.CompilerParams(vmem_limit_bytes=56 * MIB),
        cost_estimate=pl.CostEstimate(flops=20_000_000, bytes_accessed=6_000_000, transcendentals=500_000),
    )(steps)
    four = jnp.arange(4, dtype=jnp.int32)
    turns = steps[:, None] * (four[:, None] * four[None, :]).reshape(1, 16) % (scale * 4)
    phases = (2.0 * math.pi / (scale * 4)) * turns.astype(F32)
    return weights, 2.0 * jnp.concatenate([jnp.cos(phases), jnp.sin(phases)], axis=1)


def gather_kernel(x_ref, delay_ref, out_ref):
    total = x_ref[0].astype(F32)
    for r in range(1, 16):
        total = total + x_ref[r].astype(F32)
    total = total + pltpu.roll(total, 64, 1)
    top = total.astype(BF16)
    rest = (total - top.astype(F32)).astype(BF16)
    lane = lax.broadcasted_iota(jnp.int32, (64, 128), 1)
    both = jnp.where(lane < 64, top, rest)
    for q in range(4):
        for band in range(4):
            out_ref[4 * q + band, 0:16] = both[16 * q : 16 * q + 16, :]
            out_ref[4 * q + band, 16:24] = delay_ref[band]


def gather_residues(pieces, delays):
    vmem = pl.BlockSpec(memory_space=pltpu.VMEM)
    return pl.pallas_call(
        gather_kernel,
        name="residues",
        out_shape=jax.ShapeDtypeStruct((16, 24, 128), BF16),
        in_specs=[vmem] * 2,
        out_specs=vmem,
        compiler_params=pltpu.CompilerParams(vmem_limit_bytes=4 * MIB),
    )(pieces, delays)


def frame_tables():
    table = np.zeros((4, 2, 4, 4, 4, 4, 64), np.float32)
    for band in range(4):
        for m4 in range(4):
            for mb in range(4):
                row = np.full(64, -1.0 / 64.0)
                row[(16 * band + 1 + 4 * mb + m4) % 64] += 1.0
                for sub in range(4):
                    table[band, :, sub, m4, mb, sub, :] = row / math.sqrt(C)
    return table.reshape(4, 128, 256).astype(jnp.bfloat16)


def series_kernel(x_ref, tab_ref, out_ref, hot_ref, left_ref):
    series = None
    for band in range(4):
        rows = jnp.concatenate([x_ref[4 * q + band, 0:16] for q in range(4)], axis=0)
        term = lax.dot_general(rows, tab_ref[band], NN, preferred_element_type=F32)
        series = term if series is None else series + term
    ahead = lax.broadcasted_iota(jnp.int32, (64, 128), 0)
    delays = [x_ref[band, 16:24].astype(F32).astype(jnp.int32) for band in range(4)]
    for s in range(16):
        hit = (ahead + delays[s // 4][s % 4 : s % 4 + 1, :]) % 64 == 0
        hot = jnp.where(hit, 1.0, 0.0).astype(BF16)
        for th in range(4):
            cols = slice(128 * th, 128 * th + 128)
            for tile in range(4):
                to = 64 * s + 16 * tile
                at = 16 * ((tile - th) % 4)
                hot_ref[to : to + 16, cols] = hot[at : at + 16, :]
    lane = lax.broadcasted_iota(jnp.int32, (16, 128), 1) % 64
    for at in range(8):
        rows, cols = slice(16 * (at // 2), 16 * (at // 2) + 16), slice(128 * (at % 2), 128 * (at % 2) + 128)
        block = series[rows, cols].astype(BF16)
        for t in range(16):
            x = block
            if t:
                x = jnp.where(lane < 64 - t, pltpu.roll(x, 128 - t, 1), pltpu.roll(x, 64 - t, 1))
            left_ref[16 * t : 16 * t + 16, 128 * at : 128 * at + 128] = x
    out = lax.dot_general(left_ref[...], hot_ref[...], NN, preferred_element_type=F32)
    for th in range(4):
        out_ref[16 * th : 16 * th + 16] = out[:, 128 * th : 128 * th + 128].reshape(16, 16, 128)


def series(sums):
    vmem = pl.BlockSpec(memory_space=pltpu.VMEM)
    return pl.pallas_call(
        series_kernel,
        name="series",
        out_shape=jax.ShapeDtypeStruct((64, 16, 128), F32),
        in_specs=[vmem] * 2,
        out_specs=vmem,
        scratch_shapes=[pltpu.VMEM((1024, 512), BF16), pltpu.VMEM((256, 1024), BF16)],
        compiler_params=pltpu.CompilerParams(vmem_limit_bytes=8 * MIB),
        cost_estimate=pl.CostEstimate(
            flops=600_000_000, bytes_accessed=1_000_000, transcendentals=0
        ),
    )(sums, jnp.asarray(frame_tables()))


def local(voltages, steering, chan_sub, delays):
    groups, band_count = lax.axis_size("grp"), lax.axis_size("band")
    grp_at = lax.axis_index("grp")
    band_at = lax.axis_index("band")
    quarter_at = grp_at % 4
    residue = grp_at // 4

    chunks = spectra(voltages, band_at).reshape(64, 128, 128)
    turned = lax.all_to_all(chunks, "grp", split_axis=0, concat_axis=0, tiled=True)

    place = lambda r, q, b: (4 * r + q) * band_count + b
    swap = [
        (place(r, q, b), place(r, b, q))
        for r in range(groups // 4)
        for q in range(4)
        for b in range(band_count)
    ]
    quarter_subs = lax.ppermute(chan_sub, ("grp", "band"), swap)
    channels = quarter_at * 256 + 16 * jnp.arange(16, dtype=jnp.int32) + residue
    weights, east = beam_weights(channels)
    grid_at = steering[1] * 256 + steering[0]
    hot = (grid_at[:, None] == jnp.arange(1024, dtype=jnp.int32)[None, :]).astype(BF16)
    notes = jnp.transpose(delays.reshape(band_count, 128, 4), (0, 2, 1)).astype(BF16)
    notes = jnp.pad(notes, ((0, 0), (0, 4), (0, 0)))
    sums = beams(turned, east, quarter_subs, residue, weights, hot).reshape(16, 64, 128)
    planes = [[4 * r + q for r in range(groups // 4)] for q in range(4)]
    pieces = lax.all_to_all(
        sums, "grp", split_axis=0, concat_axis=0, tiled=True, axis_index_groups=planes
    )
    columns = [
        [place(r, q, b) for q in range(4) for b in range(band_count)] for r in range(groups // 4)
    ]
    every = lax.all_to_all(
        gather_residues(pieces, notes),
        ("grp", "band"),
        split_axis=0,
        concat_axis=0,
        tiled=True,
        axis_index_groups=columns,
    )
    return series(every)


def solution(mesh):
    in_specs = (P("band", "grp", None), P(), P("band"), P(None, "band"))
    out_specs = P(None, "grp", "band")
    return jax.shard_map(local, mesh=mesh, in_specs=in_specs, out_specs=out_specs, check_vma=False)
```
